32 devices in a mesh: group: 2 (over y), seq: 4 (over z), member: 4 (over x, core).
Axes of the slice: x: 2, y: 2, z: 4, core: 2. Of those that a mesh axis runs over, the one named last changes fastest.
Arguments:
- tokens: bfloat16 [8, 2048, 1024], P(('group', 'member'), 'seq'), parts along dimension 0, may hold values from -6 to 6
- input_weight: bfloat16 [1024, 3072], replicated, may hold values from -0.1875 to 0.1875
- output_weight: bfloat16 [1024, 1024], replicated, may hold values from -0.75 to 0.75
- decoder_weight: bfloat16 [1024, 128], replicated, may hold values from -0.1875 to 0.1875
- neighbours: int32 [4096, 4], P('seq'), may hold values from 0 to 2047, as said below
- observed: float32 [8192, 128], P(('group', 'seq')), parts along dimension 0, may hold values from -6 to 6
- cell_area: float32 [4096], P('seq'), may hold values from 0.3 to 3
Outputs:
- attention_cotangent: bfloat16 [8, 2048, 1024], P(('group', 'member'), 'seq'), parts along dimension 0
- output_gradient: float32 [2048, 1024], P(('group', 'seq')), parts along dimension 0
- decoder_gradient: float32 [2048, 128], P('group'), parts along dimension 0
The draws below stay inside these ranges and needn't reach their ends.
There are 2 independent parts, one for each index of `group`. The reference program is written for one: setup_inputs(seed, part) draws one part's arguments, and reference() takes and returns one part's arrays. A program takes and returns all parts, laid end to end along the dimension named above; an argument that names none is the same for every part. Nothing has to cross between parts.
Inputs may be any that keep to these rules, and one draw needn't show every extreme that they name: `neighbours`: the grid points held by index s of seq (rows s * 1024 to (s + 1) * 1024 - 1) name only tokens from s * 512 - 128 to (s + 1) * 512 + 127, cut to the tokens that exist; both ends of that range are named in every such block.
All inputs are finite; a program needn't handle non-finite values.
Results may differ from the reference program's by a relative error of at most 0.014.
Values may be sent and summed in bfloat16 or wider, within the bound.
A program may use at most 128 MiB of HBM per device.

```python
import math
import jax
import jax.numpy as jnp
from jax import lax

HEAD_DIM = 64
D = 1024
F = 128
WINDOW = 512
K = 4
REACH = 128
TOK_DEV = 512
GRID_DEV = 1024
TOKENS = 2048
GRID = 4096
MEMBERS = 4


def draw_neighbours(key, part):
    rows = jnp.arange(GRID, dtype=jnp.int32)
    owner = rows // GRID_DEV
    local_row = rows % GRID_DEV
    span = TOK_DEV + 2 * REACH
    offsets = jax.random.randint(key, (GRID, K), 0, span, dtype=jnp.int32)
    column = jnp.arange(K, dtype=jnp.int32)
    offsets = jnp.where((local_row[:, None] == 0) & (column[None, :] == 0), 0, offsets)
    offsets = jnp.where((local_row[:, None] == GRID_DEV - 1) & (column[None, :] == K - 1), span - 1, offsets)
    chosen = owner[:, None] * TOK_DEV - REACH + offsets
    return jnp.clip(chosen, 0, TOKENS - 1).astype(jnp.int32)


def levels(own_key, dims, cuts, least, top_value):
    level, own = 1.0, jax.random.fold_in(own_key, 6)
    for dim, parts in cuts:
        steps = jnp.exp(jax.random.uniform(jax.random.fold_in(own, dim), (parts,), jnp.float32, least / len(cuts), top_value / len(cuts)))
        level = level * jnp.repeat(steps, dims[dim] // parts).reshape([-1 if axis == dim else 1 for axis in range(len(dims))])
    return level


def normal_values(own_key, extent, scale, most, pieces=(), kind=jnp.bfloat16):
    gain = levels(own_key, extent, pieces, -0.22, 0.18) if pieces else 1.0
    array = jax.random.normal(own_key, extent, jnp.float32) * scale * gain
    return jnp.minimum(jnp.maximum(array, -most), most).astype(kind)


def setup_inputs(seed: int = 0, part: int = 0) -> dict:
    key_list = jax.random.split(jax.random.key(seed), 8)
    part_keys = jax.random.split(jax.random.fold_in(key_list[7], part), 8)
    return {
        "tokens": normal_values(part_keys[0], (MEMBERS, TOKENS, D), 1.0, 6.0, ((0, 4), (1, 4))),
        "input_weight": normal_values(key_list[1], (D, 3 * D), D ** -0.5, 0.1875),
        "output_weight": normal_values(key_list[2], (D, D), HEAD_DIM ** -0.5, 0.75),
        "decoder_weight": normal_values(key_list[3], (D, F), D ** -0.5, 0.1875),
        "neighbours": draw_neighbours(jax.random.fold_in(key_list[7], 71), part),
        "observed": normal_values(part_keys[5], (GRID, F), 1.0, 6.0, ((0, 4),), jnp.float32),
        "cell_area": jnp.clip(jnp.exp(math.log(3.0) - 2.3025851 * jax.random.uniform(key_list[6], (GRID,), jnp.float32) ** levels(key_list[6], (GRID,), ((0, 4),), -0.2, 0.2)), 0.3, 3.0),
    }


smooth = 0.1

def normalize(rows):
    values = rows.astype(jnp.float32)
    centre = lax.optimization_barrier(jnp.mean(values, axis=-1, keepdims=True))
    spread = lax.optimization_barrier(jnp.mean((values - centre) ** 2, axis=-1, keepdims=True))
    return ((values - centre) * lax.rsqrt(spread + 1e-05)).astype(jnp.bfloat16)

def head_norm(part):
    return (part * lax.rsqrt(lax.optimization_barrier(jnp.mean(part * part, axis=-1, keepdims=True)) + 1e-06)).astype(jnp.bfloat16)

def project(own_tokens, input_weight):
    length, width = own_tokens.shape
    heads = width // HEAD_DIM
    mixed = jnp.dot(normalize(own_tokens), input_weight, preferred_element_type=jnp.float32)
    query = head_norm(mixed[:, :width].reshape(length, heads, HEAD_DIM))
    keys = head_norm(mixed[:, width:2 * width].reshape(length, heads, HEAD_DIM))
    values = mixed[:, 2 * width:].reshape(length, heads, HEAD_DIM).astype(jnp.bfloat16)
    return (query, keys, values)

def attend(query, keys, values, key_base, total):
    length, heads, depth = query.shape
    half = (keys.shape[0] - length) // 2
    block = min(length, max(8, 512 // heads))
    count = length // block
    scale = depth ** (-0.5)

    def one_block(index):
        start = index * block
        query_block = lax.dynamic_slice_in_dim(query, start, block, 0).astype(jnp.float32)
        key_block = lax.dynamic_slice_in_dim(keys, start, block + 2 * half, 0).astype(jnp.float32)
        value_block = lax.dynamic_slice_in_dim(values, start, block + 2 * half, 0).astype(jnp.float32)
        scores = jnp.einsum('qhe,khe->hqk', query_block, key_block) * scale
        query_place = jnp.arange(block, dtype=jnp.int32)[:, None]
        key_place = jnp.arange(block + 2 * half, dtype=jnp.int32)[None, :]
        relative = key_place - query_place
        position = key_base + start + key_place
        valid = (relative >= 0) & (relative < 2 * half) & (position >= 0) & (position < total)
        weights = jnp.where(valid[None], jnp.exp(scores), 0.0)
        shares = (weights / lax.optimization_barrier(jnp.sum(weights, axis=-1, keepdims=True))).astype(jnp.bfloat16)
        return jnp.einsum('hqk,khe->qhe', shares.astype(jnp.float32), value_block).astype(jnp.bfloat16)
    result = lax.map(one_block, jnp.arange(count, dtype=jnp.int32))
    return result.reshape(length, heads, depth)

def slope(diff):
    return diff * lax.rsqrt(diff * diff + smooth * smooth)

def ensemble_cotangent(own, every, observed, cell_area):
    members = every.shape[0]
    pairs = lax.optimization_barrier(jnp.sum(slope(own[..., None, :, :] - every), axis=-3))
    single = slope(own - observed)
    return (cell_area[:, None] * (single / members - pairs / (members * (members - 1)))).astype(jnp.bfloat16)

def reference(tokens, input_weight, output_weight, decoder_weight, neighbours, observed, cell_area):
    members, total, width = tokens.shape
    half = WINDOW // 2
    fan_count = neighbours.shape[1]

    def forward(own_tokens):
        query, keys, values = project(own_tokens, input_weight)
        padding = jnp.zeros((half,) + keys.shape[1:], jnp.bfloat16)
        keys = jnp.concatenate([padding, keys, padding], axis=0)
        values = jnp.concatenate([padding, values, padding], axis=0)
        attended = attend(query, keys, values, -half, total).reshape(total, width)
        latent = (own_tokens.astype(jnp.float32) + jnp.dot(attended, output_weight, preferred_element_type=jnp.float32)).astype(jnp.bfloat16)
        pooled = (lax.optimization_barrier(jnp.sum(latent[neighbours].astype(jnp.float32), axis=1)) / fan_count).astype(jnp.bfloat16)
        fields = jnp.dot(pooled, decoder_weight, preferred_element_type=jnp.float32)
        return (attended, pooled, fields)
    attended, pooled, fields = lax.map(forward, tokens)

    def backward(carry, inputs):
        output_total, decoder_total = carry
        attended_one, pooled_one, fields_one = inputs
        field_cotangent = ensemble_cotangent(fields_one, fields, observed, cell_area)
        decoder_total = decoder_total + jnp.dot(pooled_one.T, field_cotangent, preferred_element_type=jnp.float32)
        pooled_cotangent = jnp.dot(field_cotangent, decoder_weight.T, preferred_element_type=jnp.float32)
        share = pooled_cotangent / fan_count
        latent_cotangent = jnp.zeros((total, width), jnp.float32)
        for column in range(fan_count):
            latent_cotangent = latent_cotangent.at[neighbours[:, column]].add(share)
        latent_cotangent = latent_cotangent.astype(jnp.bfloat16)
        output_total = output_total + jnp.dot(attended_one.T, latent_cotangent, preferred_element_type=jnp.float32)
        cotangent = jnp.dot(latent_cotangent, output_weight.T, preferred_element_type=jnp.float32).astype(jnp.bfloat16)
        return ((output_total, decoder_total), cotangent)
    start_carry = (jnp.zeros((width, width), jnp.float32), jnp.zeros((width, decoder_weight.shape[1]), jnp.float32))
    (output_total, decoder_total), attention_cotangent = lax.scan(backward, start_carry, (attended, pooled, fields))
    output_gradient = output_total / math.sqrt(members * total)
    decoder_gradient = decoder_total / math.sqrt(members * observed.shape[0])
    return (attention_cotangent, output_gradient, decoder_gradient)
```

```python
import functools
import math

import jax
import jax.numpy as jnp
from jax import lax
from jax.experimental import pallas as pl
from jax.experimental.pallas import tpu as pltpu
from jax.sharding import PartitionSpec as P

HEAD_DIM = 64
WINDOW = 512
REACH = 128
LANES = 128
COLS = 512

smooth = 0.1
f32 = jnp.float32
bf16 = jnp.bfloat16


def from_sides(cells, width):
    count = lax.axis_size("seq")
    rows = cells.shape[0]
    right = [(i, i + 1) for i in range(count - 1)]
    left = [(i + 1, i) for i in range(count - 1)]
    return (
        lax.ppermute(cells[rows - width :], "seq", right),
        lax.ppermute(cells[:width], "seq", left),
    )


def normalize(rows):
    values = rows.astype(f32)
    centre = jnp.mean(values, axis=-1, keepdims=True)
    values = values - centre
    spread = jnp.mean(values * values, axis=-1, keepdims=True)
    return (values * lax.rsqrt(spread + 1e-05)).astype(bf16)


def project_kernel(first, width, *refs):
    parts, weight, out, normed = refs[:-3], refs[-3], refs[-2], refs[-1]
    step = pl.program_id(0) + first

    @pl.when(pl.program_id(0) == 0)
    def _():
        row = 0
        for part in parts:
            normed[row : row + part.shape[0], :] = normalize(part[...])
            row += part.shape[0]

    mixed = jnp.dot(normed[...], weight[...], preferred_element_type=f32)
    columns = mixed.shape[1]

    @pl.when(step * columns >= 2 * width)
    def _():
        out[...] = mixed.astype(bf16)

    @pl.when(step * columns < 2 * width)
    def _():
        side = 256
        down = lax.broadcasted_iota(jnp.int32, (side, side), 0) >> 6
        across = lax.broadcasted_iota(jnp.int32, (side, side), 1) >> 6
        same = jnp.where(down == across, 1.0 / HEAD_DIM, 0.0).astype(bf16)
        scale = jnp.where(step * columns < width, HEAD_DIM**-0.5, 1.0)
        for at in range(0, columns, side):
            piece = mixed[:, at : at + side]
            mean = jnp.dot((piece * piece).astype(bf16), same, preferred_element_type=f32)
            out[:, at : at + side] = (piece * (lax.rsqrt(mean + 1e-06) * scale)).astype(bf16)


def project(parts, weight, first):
    width = weight.shape[0]
    rows = sum(part.shape[0] for part in parts)
    steps = weight.shape[1] // COLS - first
    return pl.pallas_call(
        functools.partial(project_kernel, first, width),
        grid=(steps,),
        in_specs=[pl.BlockSpec(part.shape, lambda j: (0, 0)) for part in parts]
        + [pl.BlockSpec((width, COLS), lambda j: (0, j + first))],
        out_specs=pl.BlockSpec((rows, COLS), lambda j: (0, j)),
        out_shape=jax.ShapeDtypeStruct((rows, steps * COLS), bf16),
        scratch_shapes=[pltpu.VMEM((rows, width), bf16)],
        compiler_params=pltpu.CompilerParams(vmem_limit_bytes=32 << 20),
        cost_estimate=pl.CostEstimate(
            flops=2 * rows * width * steps * COLS,
            bytes_accessed=2 * (width * steps * COLS + rows * width + rows * steps * COLS),
            transcendentals=0,
        ),
    )(*parts, weight)


def attend_kernel(
    ends, query, key_own, key_side, value_own, value_side, tokens, decoder, joint,
    out, mapped, keys, values,
):
    half = WINDOW // 2
    rows = query.shape[0]

    @pl.when(pl.program_id(0) == 0)
    def _():
        mapped[...] = jnp.dot(tokens[...], decoder[...], preferred_element_type=f32)

    keys[:half, :] = key_side[:half, :]
    keys[half : half + rows, :] = key_own[...]
    keys[half + rows :, :] = key_side[half:, :]
    first = lax.broadcasted_iota(jnp.int32, (1, LANES), 1) < HEAD_DIM
    chunks = (
        (0, value_side[:half, :], ends[0].astype(f32)),
        (half, value_own[...], 1.0),
        (half + rows, value_side[half:, :], ends[1].astype(f32)),
    )
    for at, part, exists in chunks:
        ones = jnp.full(part.shape, exists, f32).astype(bf16)
        values[0, at : at + part.shape[0], :] = jnp.where(first, part, ones)
        values[1, at : at + part.shape[0], :] = jnp.where(first, ones, part)
    block = half
    down = lax.broadcasted_iota(jnp.int32, (block, block), 0)
    across = lax.broadcasted_iota(jnp.int32, (block, block), 1)
    span = block + WINDOW
    for start in range(0, rows, block):
        own = query[start : start + block, :]
        here = keys[start : start + span, :]
        sums = []
        for head in range(2):
            part = jnp.where(first == (head == 0), own, jnp.zeros_like(own))
            scores = lax.dot_general(
                part, here, (((1,), (1,)), ((), ())), preferred_element_type=f32
            )
            weights = jnp.exp(scores)
            weights = jnp.concatenate(
                [
                    jnp.where(across >= down, weights[:, :block], 0.0).astype(bf16),
                    weights[:, block : span - block].astype(bf16),
                    jnp.where(across < down, weights[:, span - block :], 0.0).astype(bf16),
                ],
                axis=1,
            )
            total = jnp.dot(
                weights, values[head, start : start + span, :], preferred_element_type=f32
            )
            sums.append(total / pltpu.roll(total, HEAD_DIM, 1))
        result = jnp.where(first, sums[0], sums[1]).astype(bf16)
        out[start : start + block, :] = result
        mapped[start : start + block, :] += jnp.dot(
            result, joint[...], preferred_element_type=f32
        )


def attend(ends, own, side, tokens, decoder, joint):
    rows, width = tokens.shape
    steps = width // LANES
    fields = decoder.shape[1]
    wide = rows + WINDOW

    def column(array, offset):
        return pl.BlockSpec((array.shape[0], LANES), lambda j: (0, j + offset))

    return pl.pallas_call(
        attend_kernel,
        grid=(steps,),
        in_specs=[
            pl.BlockSpec(memory_space=pltpu.SMEM),
            column(own, 0),
            column(own, steps),
            column(side, 0),
            column(own, 2 * steps),
            column(side, steps),
            pl.BlockSpec(tokens.shape, lambda j: (0, 0)),
            pl.BlockSpec(decoder.shape, lambda j: (0, 0)),
            pl.BlockSpec((LANES, fields), lambda j: (j, 0)),
        ],
        out_specs=[
            pl.BlockSpec((rows, LANES), lambda j: (0, j)),
            pl.BlockSpec((rows, fields), lambda j: (0, 0)),
        ],
        out_shape=[
            jax.ShapeDtypeStruct((rows, width), bf16),
            jax.ShapeDtypeStruct((rows, fields), f32),
        ],
        scratch_shapes=[pltpu.VMEM((wide, LANES), bf16), pltpu.VMEM((2, wide, LANES), bf16)],
        compiler_params=pltpu.CompilerParams(vmem_limit_bytes=32 << 20),
    )(ends, own, own, side, own, side, tokens, decoder, joint)


def slope(diff):
    return diff * lax.rsqrt(diff * diff + smooth * smooth)


def body(tokens, input_weight, output_weight, decoder_weight, neighbours, observed, cell_area):
    own_tokens = tokens[0]
    tok_rows, width = own_tokens.shape
    fields_count = decoder_weight.shape[1]
    seq_count = lax.axis_size("seq")
    members = lax.axis_size("member")
    seq_place = lax.axis_index("seq")
    fan_count = neighbours.shape[1]
    grid_rows = neighbours.shape[0]
    wide_rows = tok_rows + 2 * REACH

    before, after = from_sides(own_tokens, WINDOW // 2)
    own = project([own_tokens], input_weight, 0)
    joint = jnp.dot(output_weight, decoder_weight, preferred_element_type=f32).astype(bf16)
    local = neighbours - (seq_place * tok_rows - REACH)
    places = jnp.arange(wide_rows, dtype=jnp.int32)
    counts = jnp.zeros((grid_rows, wide_rows), f32)
    for column in range(fan_count):
        counts = counts + (local[:, column][:, None] == places[None, :]).astype(f32)
    counts = (counts / fan_count).astype(bf16)
    side = project([before, after], input_weight, width // COLS)
    ends = jnp.stack([seq_place > 0, seq_place < seq_count - 1]).astype(jnp.int32)
    attended, mapped = attend(ends, own, side, own_tokens, decoder_weight, joint)

    mapped = mapped.astype(bf16)
    before, after = from_sides(mapped, REACH)
    mapped = jnp.concatenate([before, mapped, after], axis=0)
    every = lax.all_gather(mapped, "member", axis=0, tiled=False)
    all_fields = jnp.einsum("gt,mtf->mgf", counts, every, preferred_element_type=f32)
    fields = lax.dynamic_index_in_dim(all_fields, lax.axis_index("member"), 0, keepdims=False)
    pairs = jnp.sum(slope(fields[None] - all_fields), axis=0)
    single = slope(fields - observed)
    cotangent = (
        cell_area[:, None] * (single / members - pairs / (members * (members - 1)))
    ).astype(bf16)
    spread = lax.dot_general(
        counts, cotangent, (((0,), (0,)), ((), ())), preferred_element_type=f32
    )
    edges = jnp.concatenate([spread[:REACH], spread[REACH + tok_rows :]], axis=0)
    before, after = from_sides(edges, REACH)
    middle = spread[REACH : REACH + tok_rows]
    middle = middle.at[:REACH].add(before).at[tok_rows - REACH :].add(after).astype(bf16)
    attention_cotangent = lax.dot_general(
        middle, joint, (((1,), (1,)), ((), ())), preferred_element_type=f32
    ).astype(bf16)
    output_term = lax.dot_general(
        attended, middle, (((0,), (0,)), ((), ())), preferred_element_type=f32
    )
    decoder_term = lax.dot_general(
        own_tokens, middle, (((0,), (0,)), ((), ())), preferred_element_type=f32
    ) + lax.dot_general(
        output_weight, output_term.astype(bf16), (((0,), (0,)), ((), ())),
        preferred_element_type=f32,
    )
    both = lax.psum(
        jnp.concatenate([output_term, decoder_term], axis=1), ("seq", "member")
    )
    decoder_gradient = both[:, fields_count:] / math.sqrt(members * grid_rows * seq_count)
    rows = width // seq_count
    output_rows = lax.dynamic_slice_in_dim(both[:, :fields_count], seq_place * rows, rows, 0)
    output_gradient = lax.dot_general(
        output_rows.astype(bf16), decoder_weight, (((1,), (1,)), ((), ())),
        preferred_element_type=f32,
    ) / math.sqrt(members * tok_rows * seq_count)
    return (attention_cotangent[None], output_gradient, decoder_gradient)


def solution(mesh):
    in_specs = (
        P(("group", "member"), "seq", None),
        P(),
        P(),
        P(),
        P("seq", None),
        P(("group", "seq"), None),
        P("seq"),
    )
    out_specs = (P(("group", "member"), "seq", None), P(("group", "seq"), None), P("group", None))
    return jax.shard_map(body, mesh=mesh, in_specs=in_specs, out_specs=out_specs, check_vma=False)
```

```python
import functools
import math

import jax
import jax.numpy as jnp
from jax import lax
from jax.experimental import pallas as pl
from jax.experimental.pallas import tpu as pltpu
from jax.sharding import PartitionSpec as P

HEAD_DIM = 64
WINDOW = 512
REACH = 128
LANES = 128
COLS = 512

smooth = 0.1
f32 = jnp.float32
bf16 = jnp.bfloat16


def from_sides(cells, width):
    count = lax.axis_size("seq")
    rows = cells.shape[0]
    right = [(i, i + 1) for i in range(count - 1)]
    left = [(i + 1, i) for i in range(count - 1)]
    return (
        lax.ppermute(cells[rows - width :], "seq", right),
        lax.ppermute(cells[:width], "seq", left),
    )


def normalize(rows):
    values = rows.astype(f32)
    centre = jnp.mean(values, axis=-1, keepdims=True)
    values = values - centre
    spread = jnp.mean(values * values, axis=-1, keepdims=True)
    return (values * lax.rsqrt(spread + 1e-05)).astype(bf16)


def project_kernel(first, width, *refs):
    parts, weight, out, normed = refs[:-3], refs[-3], refs[-2], refs[-1]
    step = pl.program_id(0) + first

    @pl.when(pl.program_id(0) == 0)
    def _():
        row = 0
        for part in parts:
            normed[row : row + part.shape[0], :] = normalize(part[...])
            row += part.shape[0]

    mixed = jnp.dot(normed[...], weight[...], preferred_element_type=f32)
    columns = mixed.shape[1]

    @pl.when(step * columns >= 2 * width)
    def _():
        out[...] = mixed.astype(bf16)

    @pl.when(step * columns < 2 * width)
    def _():
        side = 256
        down = lax.broadcasted_iota(jnp.int32, (side, side), 0) >> 6
        across = lax.broadcasted_iota(jnp.int32, (side, side), 1) >> 6
        same = jnp.where(down == across, 1.0 / HEAD_DIM, 0.0).astype(bf16)
        scale = jnp.where(step * columns < width, HEAD_DIM**-0.5, 1.0)
        for at in range(0, columns, side):
            piece = mixed[:, at : at + side]
            mean = jnp.dot((piece * piece).astype(bf16), same, preferred_element_type=f32)
            out[:, at : at + side] = (piece * (lax.rsqrt(mean + 1e-06) * scale)).astype(bf16)


def project(parts, weight, first):
    width = weight.shape[0]
    rows = sum(part.shape[0] for part in parts)
    steps = weight.shape[1] // COLS - first
    return pl.pallas_call(
        functools.partial(project_kernel, first, width),
        grid=(steps,),
        in_specs=[pl.BlockSpec(part.shape, lambda j: (0, 0)) for part in parts]
        + [pl.BlockSpec((width, COLS), lambda j: (0, j + first))],
        out_specs=pl.BlockSpec((rows, COLS), lambda j: (0, j)),
        out_shape=jax.ShapeDtypeStruct((rows, steps * COLS), bf16),
        scratch_shapes=[pltpu.VMEM((rows, width), bf16)],
        compiler_params=pltpu.CompilerParams(vmem_limit_bytes=32 << 20),
        cost_estimate=pl.CostEstimate(
            flops=2 * rows * width * steps * COLS,
            bytes_accessed=2 * (width * steps * COLS + rows * width + rows * steps * COLS),
            transcendentals=0,
        ),
    )(*parts, weight)


def attend_kernel(
    ends, query, key_own, key_side, value_own, value_side, tokens, decoder, joint,
    out, mapped, keys, values,
):
    half = WINDOW // 2
    rows = query.shape[0]

    @pl.when(pl.program_id(0) == 0)
    def _():
        mapped[...] = jnp.dot(tokens[...], decoder[...], preferred_element_type=f32)

    keys[:half, :] = key_side[:half, :]
    keys[half : half + rows, :] = key_own[...]
    keys[half + rows :, :] = key_side[half:, :]
    first = lax.broadcasted_iota(jnp.int32, (1, LANES), 1) < HEAD_DIM
    chunks = (
        (0, value_side[:half, :], ends[0].astype(f32)),
        (half, value_own[...], 1.0),
        (half + rows, value_side[half:, :], ends[1].astype(f32)),
    )
    for at, part, exists in chunks:
        ones = jnp.full(part.shape, exists, f32).astype(bf16)
        values[0, at : at + part.shape[0], :] = jnp.where(first, part, ones)
        values[1, at : at + part.shape[0], :] = jnp.where(first, ones, part)
    block = half
    down = lax.broadcasted_iota(jnp.int32, (block, block), 0)
    across = lax.broadcasted_iota(jnp.int32, (block, block), 1)
    span = block + WINDOW
    for start in range(0, rows, block):
        own = query[start : start + block, :]
        here = keys[start : start + span, :]
        sums = []
        for head in range(2):
            part = jnp.where(first == (head == 0), own, jnp.zeros_like(own))
            scores = lax.dot_general(
                part, here, (((1,), (1,)), ((), ())), preferred_element_type=f32
            )
            weights = jnp.exp(scores)
            weights = jnp.concatenate(
                [
                    jnp.where(across >= down, weights[:, :block], 0.0).astype(bf16),
                    weights[:, block : span - block].astype(bf16),
                    jnp.where(across < down, weights[:, span - block :], 0.0).astype(bf16),
                ],
                axis=1,
            )
            total = jnp.dot(
                weights, values[head, start : start + span, :], preferred_element_type=f32
            )
            sums.append(total / pltpu.roll(total, HEAD_DIM, 1))
        result = jnp.where(first, sums[0], sums[1]).astype(bf16)
        out[start : start + block, :] = result
        mapped[start : start + block, :] += jnp.dot(
            result, joint[...], preferred_element_type=f32
        )


def attend(ends, own, side, tokens, decoder, joint):
    rows, width = tokens.shape
    steps = width // LANES
    fields = decoder.shape[1]
    wide = rows + WINDOW

    def column(array, offset):
        return pl.BlockSpec((array.shape[0], LANES), lambda j: (0, j + offset))

    return pl.pallas_call(
        attend_kernel,
        grid=(steps,),
        in_specs=[
            pl.BlockSpec(memory_space=pltpu.SMEM),
            column(own, 0),
            column(own, steps),
            column(side, 0),
            column(own, 2 * steps),
            column(side, steps),
            pl.BlockSpec(tokens.shape, lambda j: (0, 0)),
            pl.BlockSpec(decoder.shape, lambda j: (0, 0)),
            pl.BlockSpec((LANES, fields), lambda j: (j, 0)),
        ],
        out_specs=[
            pl.BlockSpec((rows, LANES), lambda j: (0, j)),
            pl.BlockSpec((rows, fields), lambda j: (0, 0)),
        ],
        out_shape=[
            jax.ShapeDtypeStruct((rows, width), bf16),
            jax.ShapeDtypeStruct((rows, fields), f32),
        ],
        scratch_shapes=[pltpu.VMEM((wide, LANES), bf16), pltpu.VMEM((2, wide, LANES), bf16)],
        compiler_params=pltpu.CompilerParams(vmem_limit_bytes=32 << 20),
    )(ends, own, own, side, own, side, tokens, decoder, joint)


def slope(diff):
    return diff * lax.rsqrt(diff * diff + smooth * smooth)


def copy_to(source, target, send, arrive, seq, member):
    return pltpu.make_async_remote_copy(
        src_ref=source,
        dst_ref=target,
        send_sem=send,
        recv_sem=arrive,
        device_id={"seq": seq, "member": member},
        device_id_type=pl.DeviceIdType.MESH,
    )


def tail_kernel(
    seqs, members, mapped, neighbours, area, tokens_far, attended_far, observed_far, output_far,
    middle_out, rows_out, decoder_out,
    every, counts, turned, middle, edges, edges_in, terms, terms_in, sums, sums_in, mine,
    gathered_rows, gathered, tokens, attended, observed, output_weight,
    local_sem, field_send, field_in, side_send, side_in, edge_send, edge_in, term_send, term_in,
    sum_send, sum_in, row_send, row_in, all_send, all_in,
):
    s, m = lax.axis_index("seq"), lax.axis_index("member")
    peers = seqs * members
    me = s * members + m
    tok_rows, fields = mapped.shape
    grid_rows, fan = neighbours.shape
    wide = tok_rows + 2 * REACH
    width = tokens.shape[1]
    chunk = width // peers
    own = pl.ds(REACH, tok_rows)

    def peer(step):
        flat = lax.rem(me + step, peers)
        return flat // members, lax.rem(flat, members)

    barrier = pltpu.get_barrier_semaphore()

    @pl.loop(1, peers)
    def _(step):
        seq, member = peer(step)
        pl.semaphore_signal(
            barrier, inc=1, device_id={"seq": seq, "member": member},
            device_id_type=pl.DeviceIdType.MESH,
        )

    loads = [
        pltpu.make_async_copy(far, near, local_sem.at[i])
        for i, (far, near) in enumerate(
            (
                (observed_far, observed),
                (attended_far, attended),
                (tokens_far, tokens),
                (output_far, output_weight),
            )
        )
    ]
    for load in loads:
        load.start()
    every[own, 0:fields] = mapped[...].astype(bf16)
    pl.semaphore_wait(barrier, peers - 1)

    def field_copy(step):
        lanes = pl.ds(step * fields, fields)
        return copy_to(
            every.at[own, pl.ds(0, fields)], every.at[own, lanes],
            field_send.at[step], field_in.at[step], s, lax.rem(m + step, members),
        )

    def side_copy(side, step):
        lanes = pl.ds(step * fields, fields)
        start, land, seq = ((tok_rows, 0, s + 1), (REACH, REACH + tok_rows, s - 1))[side]
        return copy_to(
            every.at[pl.ds(start, REACH), pl.ds(0, fields)],
            every.at[pl.ds(land, REACH), lanes],
            side_send.at[side, step], side_in.at[side, step], seq, lax.rem(m + step, members),
        )

    has_left, has_right = s > 0, s < seqs - 1
    for step in range(1, members):
        field_copy(step).start()

    @pl.when(has_right)
    def _():
        for step in range(members):
            side_copy(0, step).start()

    @pl.when(has_left)
    def _():
        for step in range(members):
            side_copy(1, step).start()

    @pl.when(jnp.logical_not(has_left))
    def _():
        every[:REACH, :] = jnp.zeros((REACH, members * fields), bf16)
        edges_in[0] = jnp.zeros((fields, REACH), bf16)

    @pl.when(jnp.logical_not(has_right))
    def _():
        every[wide - REACH :, :] = jnp.zeros((REACH, members * fields), bf16)
        edges_in[1] = jnp.zeros((fields, REACH), bf16)

    base = s * tok_rows - REACH
    block = 128

    @pl.loop(0, grid_rows // block)
    def _(i):
        rows = pl.ds(pl.multiple_of(i * block, block), block)
        local = neighbours[rows, :] - base
        place = lax.broadcasted_iota(jnp.int32, (block, wide), 1)
        total = jnp.zeros((block, wide), f32)
        for k in range(fan):
            total += jnp.where(local[:, k : k + 1] == place, 1.0 / fan, 0.0)
        counts[rows, :] = total.astype(bf16)

    loads[0].wait()
    for step in range(1, members):
        field_copy(step).wait()

    @pl.when(has_left)
    def _():
        for step in range(members):
            side_copy(1, step).wait_send()
            side_copy(0, step).wait_recv()

    @pl.when(has_right)
    def _():
        for step in range(members):
            side_copy(0, step).wait_send()
            side_copy(1, step).wait_recv()

    @pl.loop(0, grid_rows // block)
    def _(i):
        rows = pl.ds(pl.multiple_of(i * block, block), block)
        found = jnp.dot(counts[rows, :], every[...], preferred_element_type=f32)
        mean = found[:, :fields]
        pairs = jnp.zeros((block, fields), f32)
        for step in range(members):
            pairs += slope(mean - found[:, step * fields : (step + 1) * fields])
        single = slope(mean - observed[rows, :])
        result = area[rows, :] * (
            single * (1.0 / members) - pairs * (1.0 / (members * (members - 1)))
        )
        turned[:, rows] = result.T.astype(bf16)

    def spread(start, size):
        return jnp.dot(
            turned[...], counts[:, start : start + size], preferred_element_type=f32
        )

    edges[0] = spread(0, REACH).astype(bf16)
    edges[1] = spread(REACH + tok_rows, REACH).astype(bf16)

    def edge_copy(side):
        return copy_to(
            edges.at[side], edges_in.at[1 - side], edge_send.at[side], edge_in.at[side],
            s - 1 if side == 0 else s + 1, m,
        )

    @pl.when(has_left)
    def _():
        edge_copy(0).start()

    @pl.when(has_right)
    def _():
        edge_copy(1).start()

    middle[...] = spread(REACH, tok_rows)
    loads[1].wait()
    loads[2].wait()
    inner = middle[:, REACH : tok_rows - REACH].astype(bf16)
    output_term = jnp.dot(
        inner, attended[REACH : tok_rows - REACH, :], preferred_element_type=f32
    )

    @pl.when(has_left)
    def _():
        edge_copy(0).wait_send()
        edge_copy(1).wait_recv()

    @pl.when(has_right)
    def _():
        edge_copy(1).wait_send()
        edge_copy(0).wait_recv()

    middle[:, :REACH] += edges_in[0].astype(f32)
    middle[:, tok_rows - REACH :] += edges_in[1].astype(f32)
    whole = middle[...].astype(bf16)
    output_term += jnp.dot(whole[:, :REACH], attended[:REACH, :], preferred_element_type=f32)
    output_term += jnp.dot(
        whole[:, tok_rows - REACH :], attended[tok_rows - REACH :, :],
        preferred_element_type=f32,
    )

    def put(part, value):
        rows = value.T.astype(bf16)
        for member in range(members):
            for seq in range(seqs):
                at = (seq * members + member) * chunk
                terms[part, member, seq] = rows[at : at + chunk, :]

    def term_copy(part, step):
        member = lax.rem(m + step, members)
        return copy_to(
            terms.at[part, member], terms_in.at[part, step],
            term_send.at[part, step], term_in.at[part, step], s, member,
        )

    def sum_copy(part, step):
        seq = lax.rem(s + step, seqs)
        return copy_to(
            sums.at[part, seq], sums_in.at[part, step],
            sum_send.at[part, step], sum_in.at[part, step], seq, m,
        )

    put(0, output_term)
    for step in range(1, members):
        term_copy(0, step).start()
    decoder_term = jnp.dot(whole, tokens[...], preferred_element_type=f32)
    loads[3].wait()
    decoder_term += jnp.dot(
        output_term.astype(bf16), output_weight[...], preferred_element_type=f32
    )
    put(1, decoder_term)
    for step in range(1, members):
        term_copy(1, step).start()
    middle_out[...] = middle[...].T.astype(bf16)
    for part in range(2):
        for step in range(1, members):
            term_copy(part, step).wait()
        total = terms[part, m].astype(f32)
        for step in range(1, members):
            total += terms_in[part, step].astype(f32)
        sums[part] = total.astype(bf16)

        @pl.loop(1, seqs)
        def _(step):
            sum_copy(part, step).start()

    def row_copy(step):
        return copy_to(
            mine.at[0], gathered_rows.at[m], row_send.at[step], row_in.at[step],
            s, lax.rem(m + step, members),
        )

    def all_copy(step):
        seq, member = peer(step)
        return copy_to(
            mine.at[1], gathered.at[me], all_send.at[step], all_in.at[step], seq, member
        )

    for part in range(2):

        @pl.loop(1, seqs)
        def _(step):
            sum_copy(part, step).wait()

        total = sums[part, s].astype(f32)
        for step in range(1, seqs):
            total += sums_in[part, step].astype(f32)
        mine[part] = total.astype(bf16)
        if part == 0:
            for step in range(1, members):
                row_copy(step).start()
        else:

            @pl.loop(1, peers)
            def _(step):
                all_copy(step).start()

    gathered_rows[m] = mine[0]
    gathered[me] = mine[1]
    for step in range(1, members):
        row_copy(step).wait()
    rows_out[...] = gathered_rows[...]

    @pl.loop(1, peers)
    def _(step):
        all_copy(step).wait()

    decoder_out[...] = gathered[...]


def finish(mapped, neighbours, area, tokens, attended, observed, output_weight, seqs, members):
    tok_rows, width = tokens.shape
    fields = mapped.shape[1]
    grid_rows = neighbours.shape[0]
    wide = tok_rows + 2 * REACH
    peers = seqs * members
    chunk = width // peers
    near = pl.BlockSpec(memory_space=pltpu.VMEM)
    far = pl.BlockSpec(memory_space=pl.ANY)
    dma = pltpu.SemaphoreType.DMA
    return pl.pallas_call(
        functools.partial(tail_kernel, seqs, members),
        in_specs=[near] * 3 + [far] * 4,
        out_specs=[near] * 3,
        out_shape=[
            jax.ShapeDtypeStruct((tok_rows, fields), bf16),
            jax.ShapeDtypeStruct((members, chunk, fields), bf16),
            jax.ShapeDtypeStruct((peers, chunk, fields), bf16),
        ],
        scratch_shapes=[
            pltpu.VMEM((wide, members * fields), bf16),
            pltpu.VMEM((grid_rows, wide), bf16),
            pltpu.VMEM((fields, grid_rows), bf16),
            pltpu.VMEM((fields, tok_rows), f32),
            pltpu.VMEM((2, fields, REACH), bf16),
            pltpu.VMEM((2, fields, REACH), bf16),
            pltpu.VMEM((2, members, seqs, chunk, fields), bf16),
            pltpu.VMEM((2, members, seqs, chunk, fields), bf16),
            pltpu.VMEM((2, seqs, chunk, fields), bf16),
            pltpu.VMEM((2, seqs, chunk, fields), bf16),
            pltpu.VMEM((2, chunk, fields), bf16),
            pltpu.VMEM((members, chunk, fields), bf16),
            pltpu.VMEM((peers, chunk, fields), bf16),
            pltpu.VMEM(tokens.shape, bf16),
            pltpu.VMEM(attended.shape, bf16),
            pltpu.VMEM(observed.shape, f32),
            pltpu.VMEM(output_weight.shape, bf16),
            dma((4,)),
            dma((members,)),
            dma((members,)),
            dma((2, members)),
            dma((2, members)),
            dma((2,)),
            dma((2,)),
            dma((2, members)),
            dma((2, members)),
            dma((2, seqs)),
            dma((2, seqs)),
            dma((members,)),
            dma((members,)),
            dma((peers,)),
            dma((peers,)),
        ],
        compiler_params=pltpu.CompilerParams(
            vmem_limit_bytes=48 << 20, collective_id=0, has_side_effects=True
        ),
    )(mapped, neighbours, area, tokens, attended, observed, output_weight)


def body(tokens, input_weight, output_weight, decoder_weight, neighbours, observed, cell_area):
    own_tokens = tokens[0]
    tok_rows, width = own_tokens.shape
    fields = decoder_weight.shape[1]
    seqs = lax.axis_size("seq")
    members = lax.axis_size("member")
    seq_place = lax.axis_index("seq")
    grid_rows = neighbours.shape[0]

    before, after = from_sides(own_tokens, WINDOW // 2)
    own = project([own_tokens], input_weight, 0)
    joint = jnp.dot(output_weight, decoder_weight, preferred_element_type=f32).astype(bf16)
    side = project([before, after], input_weight, width // COLS)
    ends = jnp.stack([seq_place > 0, seq_place < seqs - 1]).astype(jnp.int32)
    attended, mapped = attend(ends, own, side, own_tokens, decoder_weight, joint)
    middle, rows, decoder_sum = finish(
        mapped, neighbours, cell_area[:, None], own_tokens, attended, observed, output_weight,
        seqs, members,
    )
    attention_cotangent = lax.dot_general(
        middle, joint, (((1,), (1,)), ((), ())), preferred_element_type=f32
    ).astype(bf16)
    output_gradient = lax.dot_general(
        rows.reshape(width // seqs, fields), decoder_weight, (((1,), (1,)), ((), ())),
        preferred_element_type=f32,
    ) * (1.0 / math.sqrt(members * tok_rows * seqs))
    decoder_gradient = decoder_sum.reshape(width, fields).astype(f32) * (
        1.0 / math.sqrt(members * grid_rows * seqs)
    )
    return (attention_cotangent[None], output_gradient, decoder_gradient)


def solution(mesh):
    in_specs = (
        P(("group", "member"), "seq", None),
        P(),
        P(),
        P(),
        P("seq", None),
        P(("group", "seq"), None),
        P("seq"),
    )
    out_specs = (P(("group", "member"), "seq", None), P(("group", "seq"), None), P("group", None))
    return jax.shard_map(body, mesh=mesh, in_specs=in_specs, out_specs=out_specs, check_vma=False)
```

```python
import functools
import math

import jax
import jax.numpy as jnp
from jax import lax
from jax.experimental import pallas as pl
from jax.experimental.pallas import tpu as pltpu
from jax.sharding import PartitionSpec as P

HEAD_DIM = 64
WINDOW = 512
REACH = 128
LANES = 128
COLS = 512

smooth = 0.1
f32 = jnp.float32
bf16 = jnp.bfloat16


def normalize(rows):
    values = rows.astype(f32)
    centre = jnp.mean(values, axis=-1, keepdims=True)
    values = values - centre
    spread = jnp.mean(values * values, axis=-1, keepdims=True)
    return (values * lax.rsqrt(spread + 1e-05)).astype(bf16)


def place_columns(mixed, scale):
    side = 256
    down = lax.broadcasted_iota(jnp.int32, (side, side), 0) >> 6
    across = lax.broadcasted_iota(jnp.int32, (side, side), 1) >> 6
    same = jnp.where(down == across, 1.0 / HEAD_DIM, 0.0).astype(bf16)
    pieces = []
    for at in range(0, mixed.shape[1], side):
        piece = mixed[:, at : at + side]
        mean = jnp.dot((piece * piece).astype(bf16), same, preferred_element_type=f32)
        pieces.append((piece * (lax.rsqrt(mean + 1e-06) * scale)).astype(bf16))
    return jnp.concatenate(pieces, axis=1)


def project(normed, weight, out, first, waits):
    width = weight.shape[0]
    for at in range(first, weight.shape[1], COLS):
        if waits:
            waits[at // COLS].wait()
        mixed = jnp.dot(normed[...], weight[:, at : at + COLS], preferred_element_type=f32)
        if at < 2 * width:
            mixed = place_columns(mixed, HEAD_DIM**-0.5 if at < width else 1.0)
        out[:, at - first : at - first + COLS] = mixed.astype(bf16)


def attend(own, side, joint, attended, mapped, keys, values, has_left, has_right):
    half = WINDOW // 2
    rows, width = attended.shape
    first = lax.broadcasted_iota(jnp.int32, (1, LANES), 1) < HEAD_DIM
    block = half
    part_rows = block // 2
    span = block + WINDOW
    part_span = part_rows + WINDOW
    down = lax.broadcasted_iota(jnp.int32, (part_rows, part_rows), 0)
    across = lax.broadcasted_iota(jnp.int32, (part_rows, part_rows), 1)
    late = across >= down
    exists = (
        jnp.where(has_left, 1.0, 0.0).astype(f32), 1.0, jnp.where(has_right, 1.0, 0.0).astype(f32)
    )

    @pl.loop(0, width // LANES)
    def _(j):
        def at(offset):
            return pl.ds(pl.multiple_of(j * LANES + offset, LANES), LANES)

        keys[:half, :] = side[:half, at(0)]
        keys[half : half + rows, :] = own[:, at(width)]
        keys[half + rows :, :] = side[half:, at(0)]
        chunks = (
            (0, side[:half, at(width)]),
            (half, own[:, at(2 * width)]),
            (half + rows, side[half:, at(width)]),
        )
        for (begin, part), there in zip(chunks, exists):
            ones = jnp.full(part.shape, there, f32).astype(bf16)
            values[0, begin : begin + part.shape[0], :] = jnp.where(first, part, ones)
            values[1, begin : begin + part.shape[0], :] = jnp.where(first, ones, part)
        for start in range(0, rows, block):
            query = own[start : start + block, at(0)]
            here = keys[start : start + span, :]
            sums = []
            for head in range(2):
                part = jnp.where(first == (head == 0), query, jnp.zeros_like(query))
                scores = lax.dot_general(
                    part, here, (((1,), (1,)), ((), ())), preferred_element_type=f32
                )
                lines = []
                for line in range(2):
                    begin = line * part_rows
                    weights = jnp.exp(
                        scores[begin : begin + part_rows, begin : begin + part_span]
                    )
                    blank = jnp.zeros((part_rows, part_rows), bf16)
                    pieces = [
                        jnp.where(late, weights[:, :part_rows], 0.0).astype(bf16),
                        weights[:, part_rows : part_span - part_rows].astype(bf16),
                        jnp.where(late, 0.0, weights[:, part_span - part_rows :]).astype(bf16),
                    ]
                    pieces = pieces + [blank] if line == 0 else [blank] + pieces
                    lines.append(jnp.concatenate(pieces, axis=1))
                total = jnp.dot(
                    jnp.concatenate(lines, axis=0),
                    values[head, start : start + span, :],
                    preferred_element_type=f32,
                )
                sums.append(total / pltpu.roll(total, HEAD_DIM, 1))
            result = jnp.where(first, sums[0], sums[1]).astype(bf16)
            attended[start : start + block, at(0)] = result
            mapped[start : start + block, :] += jnp.dot(
                result, joint[at(0), :], preferred_element_type=f32
            )


def slope(diff):
    return diff * lax.rsqrt(diff * diff + smooth * smooth)


def copy_to(source, target, send, arrive, seq, member):
    return pltpu.make_async_remote_copy(
        src_ref=source,
        dst_ref=target,
        send_sem=send,
        recv_sem=arrive,
        device_id={"seq": seq, "member": member},
        device_id_type=pl.DeviceIdType.MESH,
    )


def layer_kernel(
    seqs, members, decoder, neighbours, area, tokens_far, weight_far, observed_far, output_far,
    middle_out, rows_out, decoder_out, joint,
    every, counts, turned, middle, edges, edges_in, terms, terms_in, sums, sums_in, mine,
    gathered_rows, gathered, tokens, attended, observed, output_weight,
    weight, normed, beside, own_parts, side_parts, mapped, keys, values, halo_send, halo_in,
    local_sem, field_send, field_in, side_send, side_in, edge_send, edge_in, term_send, term_in,
    sum_send, sum_in, row_send, row_in, all_send, all_in,
):
    s, m = lax.axis_index("seq"), lax.axis_index("member")
    peers = seqs * members
    me = s * members + m
    tok_rows, fields = mapped.shape
    grid_rows, fan = neighbours.shape
    wide = tok_rows + 2 * REACH
    width = tokens.shape[1]
    chunk = width // peers
    own = pl.ds(REACH, tok_rows)

    def peer(step):
        flat = lax.rem(me + step, peers)
        return flat // members, lax.rem(flat, members)

    barrier = pltpu.get_barrier_semaphore()

    @pl.loop(1, peers)
    def _(step):
        seq, member = peer(step)
        pl.semaphore_signal(
            barrier, inc=1, device_id={"seq": seq, "member": member},
            device_id_type=pl.DeviceIdType.MESH,
        )

    columns = weight.shape[1] // COLS
    loads = [
        pltpu.make_async_copy(far, near, local_sem.at[i])
        for i, (far, near) in enumerate(
            [(tokens_far, tokens)]
            + [
                (weight_far.at[:, pl.ds(i * COLS, COLS)], weight.at[:, pl.ds(i * COLS, COLS)])
                for i in range(columns)
            ]
            + [(output_far, output_weight), (observed_far, observed)]
        )
    ]
    for load in loads:
        load.start()
    has_left, has_right = s > 0, s < seqs - 1
    half = WINDOW // 2

    def halo_copy(to_right):
        start, land, seq = (tok_rows - half, 0, s + 1) if to_right else (0, half, s - 1)
        return copy_to(
            tokens_far.at[pl.ds(start, half), :], beside.at[pl.ds(land, half), :],
            halo_send.at[to_right], halo_in.at[to_right], seq, m,
        )

    @pl.when(jnp.logical_not(has_left))
    def _():
        beside[:half, :] = jnp.zeros((half, width), bf16)

    @pl.when(jnp.logical_not(has_right))
    def _():
        beside[half:, :] = jnp.zeros((half, width), bf16)

    pl.semaphore_wait(barrier, peers - 1)

    @pl.when(has_right)
    def _():
        halo_copy(1).start()

    @pl.when(has_left)
    def _():
        halo_copy(0).start()

    loads[0].wait()
    normed[...] = normalize(tokens[...])
    project(normed, weight, own_parts, 0, loads[1 : 1 + columns])
    loads[1 + columns].wait()
    joint[...] = jnp.dot(
        output_weight[...], decoder[...], preferred_element_type=f32
    ).astype(bf16)
    mapped[...] = jnp.dot(tokens[...], decoder[...], preferred_element_type=f32)
    base = s * tok_rows - REACH
    block = 128

    @pl.loop(0, grid_rows // block)
    def _(i):
        rows = pl.ds(pl.multiple_of(i * block, block), block)
        local = neighbours[rows, :] - base
        place = lax.broadcasted_iota(jnp.int32, (block, wide), 1)
        total = jnp.zeros((block, wide), f32)
        for k in range(fan):
            total += jnp.where(local[:, k : k + 1] == place, 1.0 / fan, 0.0)
        counts[rows, :] = total.astype(bf16)

    @pl.when(has_left)
    def _():
        halo_copy(0).wait_send()
        halo_copy(1).wait_recv()

    @pl.when(has_right)
    def _():
        halo_copy(1).wait_send()
        halo_copy(0).wait_recv()

    normed[...] = normalize(beside[...])
    project(normed, weight, side_parts, width, None)
    attend(
        own_parts, side_parts, joint, attended, mapped, keys, values, has_left, has_right
    )
    every[own, 0:fields] = mapped[...].astype(bf16)

    def field_copy(step):
        lanes = pl.ds(step * fields, fields)
        return copy_to(
            every.at[own, pl.ds(0, fields)], every.at[own, lanes],
            field_send.at[step], field_in.at[step], s, lax.rem(m + step, members),
        )

    def side_copy(side, step):
        lanes = pl.ds(step * fields, fields)
        start, land, seq = ((tok_rows, 0, s + 1), (REACH, REACH + tok_rows, s - 1))[side]
        return copy_to(
            every.at[pl.ds(start, REACH), pl.ds(0, fields)],
            every.at[pl.ds(land, REACH), lanes],
            side_send.at[side, step], side_in.at[side, step], seq, lax.rem(m + step, members),
        )

    for step in range(1, members):
        field_copy(step).start()

    @pl.when(has_right)
    def _():
        for step in range(members):
            side_copy(0, step).start()

    @pl.when(has_left)
    def _():
        for step in range(members):
            side_copy(1, step).start()

    @pl.when(jnp.logical_not(has_left))
    def _():
        every[:REACH, :] = jnp.zeros((REACH, members * fields), bf16)
        edges_in[0] = jnp.zeros((fields, REACH), bf16)

    @pl.when(jnp.logical_not(has_right))
    def _():
        every[wide - REACH :, :] = jnp.zeros((REACH, members * fields), bf16)
        edges_in[1] = jnp.zeros((fields, REACH), bf16)

    loads[2 + columns].wait()
    for step in range(1, members):
        field_copy(step).wait()

    @pl.when(has_left)
    def _():
        for step in range(members):
            side_copy(1, step).wait_send()
            side_copy(0, step).wait_recv()

    @pl.when(has_right)
    def _():
        for step in range(members):
            side_copy(0, step).wait_send()
            side_copy(1, step).wait_recv()

    @pl.loop(0, grid_rows // block)
    def _(i):
        rows = pl.ds(pl.multiple_of(i * block, block), block)
        found = jnp.dot(counts[rows, :], every[...], preferred_element_type=f32)
        mean = found[:, :fields]
        pairs = jnp.zeros((block, fields), f32)
        for step in range(members):
            pairs += slope(mean - found[:, step * fields : (step + 1) * fields])
        single = slope(mean - observed[rows, :])
        result = area[rows, :] * (
            single * (1.0 / members) - pairs * (1.0 / (members * (members - 1)))
        )
        turned[:, rows] = result.T.astype(bf16)

    def spread(start, size):
        return jnp.dot(
            turned[...], counts[:, start : start + size], preferred_element_type=f32
        )

    edges[0] = spread(0, REACH).astype(bf16)
    edges[1] = spread(REACH + tok_rows, REACH).astype(bf16)

    def edge_copy(side):
        return copy_to(
            edges.at[side], edges_in.at[1 - side], edge_send.at[side], edge_in.at[side],
            s - 1 if side == 0 else s + 1, m,
        )

    @pl.when(has_left)
    def _():
        edge_copy(0).start()

    @pl.when(has_right)
    def _():
        edge_copy(1).start()

    middle[...] = spread(REACH, tok_rows)
    inner = middle[:, REACH : tok_rows - REACH].astype(bf16)
    output_term = jnp.dot(
        inner, attended[REACH : tok_rows - REACH, :], preferred_element_type=f32
    )

    @pl.when(has_left)
    def _():
        edge_copy(0).wait_send()
        edge_copy(1).wait_recv()

    @pl.when(has_right)
    def _():
        edge_copy(1).wait_send()
        edge_copy(0).wait_recv()

    middle[:, :REACH] += edges_in[0].astype(f32)
    middle[:, tok_rows - REACH :] += edges_in[1].astype(f32)
    whole = middle[...].astype(bf16)
    output_term += jnp.dot(whole[:, :REACH], attended[:REACH, :], preferred_element_type=f32)
    output_term += jnp.dot(
        whole[:, tok_rows - REACH :], attended[tok_rows - REACH :, :],
        preferred_element_type=f32,
    )

    def put(part, value):
        rows = value.T.astype(bf16)
        for member in range(members):
            for seq in range(seqs):
                at = (seq * members + member) * chunk
                terms[part, member, seq] = rows[at : at + chunk, :]

    def term_copy(part, step):
        member = lax.rem(m + step, members)
        return copy_to(
            terms.at[part, member], terms_in.at[part, step],
            term_send.at[part, step], term_in.at[part, step], s, member,
        )

    def sum_copy(part, step):
        seq = lax.rem(s + step, seqs)
        return copy_to(
            sums.at[part, seq], sums_in.at[part, step],
            sum_send.at[part, step], sum_in.at[part, step], seq, m,
        )

    put(0, output_term)
    for step in range(1, members):
        term_copy(0, step).start()
    decoder_term = jnp.dot(whole, tokens[...], preferred_element_type=f32)
    decoder_term += jnp.dot(
        output_term.astype(bf16), output_weight[...], preferred_element_type=f32
    )
    put(1, decoder_term)
    for step in range(1, members):
        term_copy(1, step).start()
    middle_out[...] = middle[...].T.astype(bf16)
    for part in range(2):
        for step in range(1, members):
            term_copy(part, step).wait()
        total = terms[part, m].astype(f32)
        for step in range(1, members):
            total += terms_in[part, step].astype(f32)
        sums[part] = total.astype(bf16)

        @pl.loop(1, seqs)
        def _(step):
            sum_copy(part, step).start()

    def row_copy(step):
        return copy_to(
            mine.at[0], gathered_rows.at[m], row_send.at[step], row_in.at[step],
            s, lax.rem(m + step, members),
        )

    def all_copy(step):
        seq, member = peer(step)
        return copy_to(
            mine.at[1], gathered.at[me], all_send.at[step], all_in.at[step], seq, member
        )

    for part in range(2):

        @pl.loop(1, seqs)
        def _(step):
            sum_copy(part, step).wait()

        total = sums[part, s].astype(f32)
        for step in range(1, seqs):
            total += sums_in[part, step].astype(f32)
        mine[part] = total.astype(bf16)
        if part == 0:
            for step in range(1, members):
                row_copy(step).start()
        else:

            @pl.loop(1, peers)
            def _(step):
                all_copy(step).start()

    gathered_rows[m] = mine[0]
    gathered[me] = mine[1]
    for step in range(1, members):
        row_copy(step).wait()
    rows_out[...] = gathered_rows[...]

    @pl.loop(1, peers)
    def _(step):
        all_copy(step).wait()

    decoder_out[...] = gathered[...]


def layer(decoder, neighbours, area, tokens, weight, observed, output_weight, seqs, members):
    tok_rows, width = tokens.shape
    fields = decoder.shape[1]
    grid_rows = neighbours.shape[0]
    wide = tok_rows + 2 * REACH
    peers = seqs * members
    chunk = width // peers
    near = pl.BlockSpec(memory_space=pltpu.VMEM)
    far = pl.BlockSpec(memory_space=pl.ANY)
    dma = pltpu.SemaphoreType.DMA
    return pl.pallas_call(
        functools.partial(layer_kernel, seqs, members),
        in_specs=[near] * 3 + [far] * 4,
        out_specs=[near] * 4,
        out_shape=[
            jax.ShapeDtypeStruct((tok_rows, fields), bf16),
            jax.ShapeDtypeStruct((members, chunk, fields), bf16),
            jax.ShapeDtypeStruct((peers, chunk, fields), bf16),
            jax.ShapeDtypeStruct((width, fields), bf16),
        ],
        scratch_shapes=[
            pltpu.VMEM((wide, members * fields), bf16),
            pltpu.VMEM((grid_rows, wide), bf16),
            pltpu.VMEM((fields, grid_rows), bf16),
            pltpu.VMEM((fields, tok_rows), f32),
            pltpu.VMEM((2, fields, REACH), bf16),
            pltpu.VMEM((2, fields, REACH), bf16),
            pltpu.VMEM((2, members, seqs, chunk, fields), bf16),
            pltpu.VMEM((2, members, seqs, chunk, fields), bf16),
            pltpu.VMEM((2, seqs, chunk, fields), bf16),
            pltpu.VMEM((2, seqs, chunk, fields), bf16),
            pltpu.VMEM((2, chunk, fields), bf16),
            pltpu.VMEM((members, chunk, fields), bf16),
            pltpu.VMEM((peers, chunk, fields), bf16),
            pltpu.VMEM(tokens.shape, bf16),
            pltpu.VMEM(tokens.shape, bf16),
            pltpu.VMEM(observed.shape, f32),
            pltpu.VMEM(output_weight.shape, bf16),
            pltpu.VMEM(weight.shape, bf16),
            pltpu.VMEM(tokens.shape, bf16),
            pltpu.VMEM((WINDOW, width), bf16),
            pltpu.VMEM((tok_rows, 3 * width), bf16),
            pltpu.VMEM((WINDOW, 2 * width), bf16),
            pltpu.VMEM((tok_rows, fields), f32),
            pltpu.VMEM((tok_rows + WINDOW, LANES), bf16),
            pltpu.VMEM((2, tok_rows + WINDOW, LANES), bf16),
            dma((2,)),
            dma((2,)),
            dma((3 + weight.shape[1] // COLS,)),
            dma((members,)),
            dma((members,)),
            dma((2, members)),
            dma((2, members)),
            dma((2,)),
            dma((2,)),
            dma((2, members)),
            dma((2, members)),
            dma((2, seqs)),
            dma((2, seqs)),
            dma((members,)),
            dma((members,)),
            dma((peers,)),
            dma((peers,)),
        ],
        compiler_params=pltpu.CompilerParams(
            vmem_limit_bytes=56 << 20, collective_id=0, has_side_effects=True
        ),
    )(decoder, neighbours, area, tokens, weight, observed, output_weight)


def body(tokens, input_weight, output_weight, decoder_weight, neighbours, observed, cell_area):
    own_tokens = tokens[0]
    tok_rows, width = own_tokens.shape
    fields = decoder_weight.shape[1]
    seqs = lax.axis_size("seq")
    members = lax.axis_size("member")
    grid_rows = neighbours.shape[0]
    middle, rows, decoder_sum, joint = layer(
        decoder_weight, neighbours, cell_area[:, None], own_tokens, input_weight, observed,
        output_weight, seqs, members,
    )
    attention_cotangent = lax.dot_general(
        middle, joint, (((1,), (1,)), ((), ())), preferred_element_type=f32
    ).astype(bf16)
    output_gradient = lax.dot_general(
        rows.reshape(width // seqs, fields), decoder_weight, (((1,), (1,)), ((), ())),
        preferred_element_type=f32,
    ) * (1.0 / math.sqrt(members * tok_rows * seqs))
    decoder_gradient = decoder_sum.reshape(width, fields).astype(f32) * (
        1.0 / math.sqrt(members * grid_rows * seqs)
    )
    return (attention_cotangent[None], output_gradient, decoder_gradient)


def solution(mesh):
    in_specs = (
        P(("group", "member"), "seq", None),
        P(),
        P(),
        P(),
        P("seq", None),
        P(("group", "seq"), None),
        P("seq"),
    )
    out_specs = (P(("group", "member"), "seq", None), P(("group", "seq"), None), P("group", None))
    return jax.shard_map(body, mesh=mesh, in_specs=in_specs, out_specs=out_specs, check_vma=False)
```

```python
import functools
import math

import jax
import jax.numpy as jnp
from jax import lax
from jax.experimental import pallas as pl
from jax.experimental.pallas import tpu as pltpu
from jax.sharding import PartitionSpec as P

HEAD_DIM = 64
WINDOW = 512
REACH = 128
LANES = 128
COLS = 512

smooth = 0.1
f32 = jnp.float32
bf16 = jnp.bfloat16


def normalize(rows):
    values = rows.astype(f32)
    centre = jnp.mean(values, axis=-1, keepdims=True)
    values = values - centre
    spread = jnp.mean(values * values, axis=-1, keepdims=True)
    return (values * lax.rsqrt(spread + 1e-05)).astype(bf16)


def place_columns(mixed, scale):
    side = 256
    down = lax.broadcasted_iota(jnp.int32, (side, side), 0) >> 6
    across = lax.broadcasted_iota(jnp.int32, (side, side), 1) >> 6
    same = jnp.where(down == across, 1.0 / HEAD_DIM, 0.0).astype(bf16)
    pieces = []
    for at in range(0, mixed.shape[1], side):
        piece = mixed[:, at : at + side]
        mean = jnp.dot((piece * piece).astype(bf16), same, preferred_element_type=f32)
        pieces.append((piece * (lax.rsqrt(mean + 1e-06) * scale)).astype(bf16))
    return jnp.concatenate(pieces, axis=1)


def project(normed, weight, out, first, waits):
    width = weight.shape[0]
    for at in range(first, weight.shape[1], COLS):
        if waits:
            waits[at // COLS].wait()
        mixed = jnp.dot(normed[...], weight[:, at : at + COLS], preferred_element_type=f32)
        if at < 2 * width:
            mixed = place_columns(mixed, HEAD_DIM**-0.5 if at < width else 1.0)
        out[:, at - first : at - first + COLS] = mixed.astype(bf16)


def attend(index, own, side, joint, attended, mapped, keys, values, there):
    half = WINDOW // 2
    rows, width = attended.shape
    first = lax.broadcasted_iota(jnp.int32, (1, LANES), 1) < HEAD_DIM
    block = half
    part_rows = block // 2
    part_span = part_rows + WINDOW
    down = lax.broadcasted_iota(jnp.int32, (part_rows, part_rows), 0)
    across = lax.broadcasted_iota(jnp.int32, (part_rows, part_rows), 1)
    late = across >= down
    start = index * block
    outside = pl.ds(index * half, half)
    shift = (half, 0)[index]
    apart = (0, rows)[index]
    there = jnp.where(there, 1.0, 0.0).astype(f32)

    @pl.loop(0, width // LANES)
    def _(j):
        def at(offset):
            return pl.ds(pl.multiple_of(j * LANES + offset, LANES), LANES)

        keys[shift : shift + rows, :] = own[:, at(width)]
        keys[apart : apart + half, :] = side[outside, at(0)]
        chunks = (
            (shift, own[:, at(2 * width)], 1.0),
            (apart, side[outside, at(width)], there),
        )
        for begin, part, real in chunks:
            ones = jnp.full(part.shape, real, f32).astype(bf16)
            values[0, begin : begin + part.shape[0], :] = jnp.where(first, part, ones)
            values[1, begin : begin + part.shape[0], :] = jnp.where(first, ones, part)
        query = own[start : start + block, at(0)]
        here = keys[...]
        sums = []
        for head in range(2):
            part = jnp.where(first == (head == 0), query, jnp.zeros_like(query))
            scores = lax.dot_general(
                part, here, (((1,), (1,)), ((), ())), preferred_element_type=f32
            )
            lines = []
            for line in range(2):
                begin = line * part_rows
                weights = jnp.exp(
                    scores[begin : begin + part_rows, begin : begin + part_span]
                )
                blank = jnp.zeros((part_rows, part_rows), bf16)
                pieces = [
                    jnp.where(late, weights[:, :part_rows], 0.0).astype(bf16),
                    weights[:, part_rows : part_span - part_rows].astype(bf16),
                    jnp.where(late, 0.0, weights[:, part_span - part_rows :]).astype(bf16),
                ]
                pieces = pieces + [blank] if line == 0 else [blank] + pieces
                lines.append(jnp.concatenate(pieces, axis=1))
            total = jnp.dot(
                jnp.concatenate(lines, axis=0),
                values[head],
                preferred_element_type=f32,
            )
            sums.append(total / pltpu.roll(total, HEAD_DIM, 1))
        result = jnp.where(first, sums[0], sums[1]).astype(bf16)
        attended[start : start + block, at(0)] = result
        mapped[start : start + block, :] += jnp.dot(
            result, joint[at(0), :], preferred_element_type=f32
        )


def slope(diff):
    return diff * lax.rsqrt(diff * diff + smooth * smooth)


def copy_to(source, target, send, arrive, seq, member):
    return pltpu.make_async_remote_copy(
        src_ref=source,
        dst_ref=target,
        send_sem=send,
        recv_sem=arrive,
        device_id={"seq": seq, "member": member},
        device_id_type=pl.DeviceIdType.MESH,
    )


def layer_kernel(
    seqs, members, decoder, neighbours, area, tokens_far, weight_far, observed_far, output_far,
    middle_out, rows_out, decoder_out, joint,
    every, counts, turned, middle, edges, edges_in, terms, terms_in, sums, sums_in, mine,
    gathered_rows, gathered, tokens, attended, observed, output_weight,
    weight, normed, beside, own_parts, side_parts, mapped, keys, values, seen,
    halo_send, halo_in,
    local_sem, field_send, field_in, side_send, side_in, edge_send, edge_in, term_send, term_in,
    sum_send, sum_in, row_send, row_in, all_send, all_in,
):
    s, m = lax.axis_index("seq"), lax.axis_index("member")
    peers = seqs * members
    me = s * members + m
    tok_rows, fields = mapped.shape
    fan, grid_rows = neighbours.shape
    wide = tok_rows + 2 * REACH
    width = tokens.shape[1]
    chunk = width // peers

    def peer(step):
        flat = lax.rem(me + step, peers)
        return flat // members, lax.rem(flat, members)

    barrier = pltpu.get_barrier_semaphore()

    @pl.loop(1, peers)
    def _(step):
        seq, member = peer(step)
        pl.semaphore_signal(
            barrier, inc=1, device_id={"seq": seq, "member": member},
            device_id_type=pl.DeviceIdType.MESH,
        )

    columns = weight.shape[1] // COLS
    loads = [
        pltpu.make_async_copy(far, near, local_sem.at[i])
        for i, (far, near) in enumerate(
            [(tokens_far, tokens)]
            + [
                (weight_far.at[:, pl.ds(i * COLS, COLS)], weight.at[:, pl.ds(i * COLS, COLS)])
                for i in range(columns)
            ]
            + [(output_far, output_weight), (observed_far, observed)]
        )
    ]
    for load in loads:
        load.start()
    has_left, has_right = s > 0, s < seqs - 1
    half = WINDOW // 2

    def halo_copy(to_right):
        start, land, seq = (tok_rows - half, 0, s + 1) if to_right else (0, half, s - 1)
        return copy_to(
            tokens_far.at[pl.ds(start, half), :], beside.at[pl.ds(land, half), :],
            halo_send.at[to_right], halo_in.at[to_right], seq, m,
        )

    @pl.when(jnp.logical_not(has_left))
    def _():
        beside[:half, :] = jnp.zeros((half, width), bf16)

    @pl.when(jnp.logical_not(has_right))
    def _():
        beside[half:, :] = jnp.zeros((half, width), bf16)

    pl.semaphore_wait(barrier, peers - 1)

    @pl.when(has_right)
    def _():
        halo_copy(1).start()

    @pl.when(has_left)
    def _():
        halo_copy(0).start()

    loads[0].wait()
    normed[...] = normalize(tokens[...])
    project(normed, weight, own_parts, 0, loads[1 : 1 + columns])
    loads[1 + columns].wait()
    joint[...] = jnp.dot(
        output_weight[...], decoder[...], preferred_element_type=f32
    ).astype(bf16)
    mapped[...] = jnp.dot(tokens[...], decoder[...], preferred_element_type=f32)
    base = s * tok_rows - REACH
    block = 128
    loads[2 + columns].wait()

    @pl.loop(0, grid_rows // block)
    def _(i):
        cells = pl.ds(pl.multiple_of(i * block, block), block)
        local = neighbours[:, cells] - base
        place = lax.broadcasted_iota(jnp.int32, (wide, block), 0)
        total = jnp.zeros((wide, block), f32)
        for k in range(fan):
            total += jnp.where(local[k : k + 1, :] == place, 1.0 / fan, 0.0)
        counts[:, cells] = total.astype(bf16)
        seen[:, cells] = observed[cells, :].T

    @pl.when(has_left)
    def _():
        halo_copy(0).wait_send()
        halo_copy(1).wait_recv()

    @pl.when(has_right)
    def _():
        halo_copy(1).wait_send()
        halo_copy(0).wait_recv()

    normed[...] = normalize(beside[...])
    project(normed, weight, side_parts, width, None)
    def field_copy(index, step):
        cells = pl.ds(REACH + index * half, half)
        return copy_to(
            every.at[pl.ds(0, fields), cells], every.at[pl.ds(step * fields, fields), cells],
            field_send.at[index, step], field_in.at[index, step], s, lax.rem(m + step, members),
        )

    def side_copy(side, step):
        start, land, seq = ((tok_rows, 0, s + 1), (REACH, REACH + tok_rows, s - 1))[side]
        return copy_to(
            every.at[pl.ds(0, fields), pl.ds(start, REACH)],
            every.at[pl.ds(step * fields, fields), pl.ds(land, REACH)],
            side_send.at[side, step], side_in.at[side, step], seq, lax.rem(m + step, members),
        )

    for index in range(2):
        attend(
            index, own_parts, side_parts, joint, attended, mapped, keys, values,
            (has_left, has_right)[index],
        )
        at = index * half
        every[:fields, REACH + at : REACH + at + half] = (
            mapped[at : at + half, :].T.astype(bf16)
        )
        for step in range(1, members):
            field_copy(index, step).start()

        @pl.when((has_left, has_right)[index])
        def _():
            for step in range(members):
                side_copy(1 - index, step).start()

    @pl.when(jnp.logical_not(has_left))
    def _():
        every[:, :REACH] = jnp.zeros((members * fields, REACH), bf16)
        edges_in[0] = jnp.zeros((fields, REACH), bf16)

    @pl.when(jnp.logical_not(has_right))
    def _():
        every[:, wide - REACH :] = jnp.zeros((members * fields, REACH), bf16)
        edges_in[1] = jnp.zeros((fields, REACH), bf16)

    for index in range(2):
        for step in range(1, members):
            field_copy(index, step).wait()

    @pl.when(has_left)
    def _():
        for step in range(members):
            side_copy(1, step).wait_send()
            side_copy(0, step).wait_recv()

    @pl.when(has_right)
    def _():
        for step in range(members):
            side_copy(0, step).wait_send()
            side_copy(1, step).wait_recv()

    block = 256

    @pl.loop(0, grid_rows // block)
    def _(i):
        cells = pl.ds(pl.multiple_of(i * block, block), block)
        found = jnp.dot(every[...], counts[:, cells], preferred_element_type=f32)
        mean = found[:fields, :]
        pairs = jnp.zeros((fields, block), f32)
        for step in range(members):
            pairs += slope(mean - found[step * fields : (step + 1) * fields, :])
        single = slope(mean - seen[:, cells])
        turned[:, cells] = (
            area[:, cells]
            * (single * (1.0 / members) - pairs * (1.0 / (members * (members - 1))))
        ).astype(bf16)

    def spread(start, size):
        return lax.dot_general(
            turned[...], counts[start : start + size, :], (((1,), (1,)), ((), ())),
            preferred_element_type=f32,
        )

    edges[0] = spread(0, REACH).astype(bf16)
    edges[1] = spread(REACH + tok_rows, REACH).astype(bf16)

    def edge_copy(side):
        return copy_to(
            edges.at[side], edges_in.at[1 - side], edge_send.at[side], edge_in.at[side],
            s - 1 if side == 0 else s + 1, m,
        )

    @pl.when(has_left)
    def _():
        edge_copy(0).start()

    @pl.when(has_right)
    def _():
        edge_copy(1).start()

    middle[...] = spread(REACH, tok_rows)
    inner = middle[:, REACH : tok_rows - REACH].astype(bf16)
    output_term = jnp.dot(
        inner, attended[REACH : tok_rows - REACH, :], preferred_element_type=f32
    )

    @pl.when(has_left)
    def _():
        edge_copy(0).wait_send()
        edge_copy(1).wait_recv()

    @pl.when(has_right)
    def _():
        edge_copy(1).wait_send()
        edge_copy(0).wait_recv()

    middle[:, :REACH] += edges_in[0].astype(f32)
    middle[:, tok_rows - REACH :] += edges_in[1].astype(f32)
    whole = middle[...].astype(bf16)
    output_term += jnp.dot(whole[:, :REACH], attended[:REACH, :], preferred_element_type=f32)
    output_term += jnp.dot(
        whole[:, tok_rows - REACH :], attended[tok_rows - REACH :, :],
        preferred_element_type=f32,
    )

    def put(part, value):
        rows = value.T.astype(bf16)
        for member in range(members):
            for seq in range(seqs):
                at = (seq * members + member) * chunk
                terms[part, member, seq] = rows[at : at + chunk, :]

    def term_copy(part, step):
        member = lax.rem(m + step, members)
        return copy_to(
            terms.at[part, member], terms_in.at[part, step],
            term_send.at[part, step], term_in.at[part, step], s, member,
        )

    def sum_copy(part, step):
        seq = lax.rem(s + step, seqs)
        return copy_to(
            sums.at[part, seq], sums_in.at[part, step],
            sum_send.at[part, step], sum_in.at[part, step], seq, m,
        )

    put(0, output_term)
    for step in range(1, members):
        term_copy(0, step).start()
    decoder_term = jnp.dot(whole, tokens[...], preferred_element_type=f32)
    decoder_term += jnp.dot(
        output_term.astype(bf16), output_weight[...], preferred_element_type=f32
    )
    put(1, decoder_term)
    for step in range(1, members):
        term_copy(1, step).start()
    middle_out[...] = middle[...].T.astype(bf16)
    for part in range(2):
        for step in range(1, members):
            term_copy(part, step).wait()
        total = terms[part, m].astype(f32)
        for step in range(1, members):
            total += terms_in[part, step].astype(f32)
        sums[part] = total.astype(bf16)

        @pl.loop(1, seqs)
        def _(step):
            sum_copy(part, step).start()

    def row_copy(step):
        return copy_to(
            mine.at[0], gathered_rows.at[m], row_send.at[step], row_in.at[step],
            s, lax.rem(m + step, members),
        )

    def all_copy(step):
        seq, member = peer(step)
        return copy_to(
            mine.at[1], gathered.at[me], all_send.at[step], all_in.at[step], seq, member
        )

    for part in range(2):

        @pl.loop(1, seqs)
        def _(step):
            sum_copy(part, step).wait()

        total = sums[part, s].astype(f32)
        for step in range(1, seqs):
            total += sums_in[part, step].astype(f32)
        mine[part] = total.astype(bf16)
        if part == 0:
            for step in range(1, members):
                row_copy(step).start()
        else:

            @pl.loop(1, peers)
            def _(step):
                all_copy(step).start()

    gathered_rows[m] = mine[0]
    gathered[me] = mine[1]
    for step in range(1, members):
        row_copy(step).wait()
    rows_out[...] = gathered_rows[...]

    @pl.loop(1, peers)
    def _(step):
        all_copy(step).wait()

    decoder_out[...] = gathered[...]


def layer(decoder, neighbours, area, tokens, weight, observed, output_weight, seqs, members):
    tok_rows, width = tokens.shape
    fields = decoder.shape[1]
    grid_rows = neighbours.shape[1]
    wide = tok_rows + 2 * REACH
    peers = seqs * members
    chunk = width // peers
    near = pl.BlockSpec(memory_space=pltpu.VMEM)
    far = pl.BlockSpec(memory_space=pl.ANY)
    dma = pltpu.SemaphoreType.DMA
    return pl.pallas_call(
        functools.partial(layer_kernel, seqs, members),
        in_specs=[near] * 3 + [far] * 4,
        out_specs=[near] * 4,
        out_shape=[
            jax.ShapeDtypeStruct((tok_rows, fields), bf16),
            jax.ShapeDtypeStruct((members, chunk, fields), bf16),
            jax.ShapeDtypeStruct((peers, chunk, fields), bf16),
            jax.ShapeDtypeStruct((width, fields), bf16),
        ],
        scratch_shapes=[
            pltpu.VMEM((members * fields, wide), bf16),
            pltpu.VMEM((wide, grid_rows), bf16),
            pltpu.VMEM((fields, grid_rows), bf16),
            pltpu.VMEM((fields, tok_rows), f32),
            pltpu.VMEM((2, fields, REACH), bf16),
            pltpu.VMEM((2, fields, REACH), bf16),
            pltpu.VMEM((2, members, seqs, chunk, fields), bf16),
            pltpu.VMEM((2, members, seqs, chunk, fields), bf16),
            pltpu.VMEM((2, seqs, chunk, fields), bf16),
            pltpu.VMEM((2, seqs, chunk, fields), bf16),
            pltpu.VMEM((2, chunk, fields), bf16),
            pltpu.VMEM((members, chunk, fields), bf16),
            pltpu.VMEM((peers, chunk, fields), bf16),
            pltpu.VMEM(tokens.shape, bf16),
            pltpu.VMEM(tokens.shape, bf16),
            pltpu.VMEM(observed.shape, f32),
            pltpu.VMEM(output_weight.shape, bf16),
            pltpu.VMEM(weight.shape, bf16),
            pltpu.VMEM(tokens.shape, bf16),
            pltpu.VMEM((WINDOW, width), bf16),
            pltpu.VMEM((tok_rows, 3 * width), bf16),
            pltpu.VMEM((WINDOW, 2 * width), bf16),
            pltpu.VMEM((tok_rows, fields), f32),
            pltpu.VMEM((WINDOW // 2 + WINDOW, LANES), bf16),
            pltpu.VMEM((2, WINDOW // 2 + WINDOW, LANES), bf16),
            pltpu.VMEM((fields, grid_rows), f32),
            dma((2,)),
            dma((2,)),
            dma((3 + weight.shape[1] // COLS,)),
            dma((2, members)),
            dma((2, members)),
            dma((2, members)),
            dma((2, members)),
            dma((2,)),
            dma((2,)),
            dma((2, members)),
            dma((2, members)),
            dma((2, seqs)),
            dma((2, seqs)),
            dma((members,)),
            dma((members,)),
            dma((peers,)),
            dma((peers,)),
        ],
        compiler_params=pltpu.CompilerParams(
            vmem_limit_bytes=56 << 20, collective_id=0, has_side_effects=True
        ),
    )(decoder, neighbours, area, tokens, weight, observed, output_weight)


def body(tokens, input_weight, output_weight, decoder_weight, neighbours, observed, cell_area):
    own_tokens = tokens[0]
    tok_rows, width = own_tokens.shape
    fields = decoder_weight.shape[1]
    seqs = lax.axis_size("seq")
    members = lax.axis_size("member")
    grid_rows = neighbours.shape[0]
    middle, rows, decoder_sum, joint = layer(
        decoder_weight, neighbours.T, cell_area[None, :], own_tokens, input_weight, observed,
        output_weight, seqs, members,
    )
    attention_cotangent = lax.dot_general(
        middle, joint, (((1,), (1,)), ((), ())), preferred_element_type=f32
    ).astype(bf16)
    output_gradient = lax.dot_general(
        rows.reshape(width // seqs, fields), decoder_weight, (((1,), (1,)), ((), ())),
        preferred_element_type=f32,
    ) * (1.0 / math.sqrt(members * tok_rows * seqs))
    decoder_gradient = decoder_sum.reshape(width, fields).astype(f32) * (
        1.0 / math.sqrt(members * grid_rows * seqs)
    )
    return (attention_cotangent[None], output_gradient, decoder_gradient)


def solution(mesh):
    in_specs = (
        P(("group", "member"), "seq", None),
        P(),
        P(),
        P(),
        P("seq", None),
        P(("group", "seq"), None),
        P("seq"),
    )
    out_specs = (P(("group", "member"), "seq", None), P(("group", "seq"), None), P("group", None))
    return jax.shard_map(body, mesh=mesh, in_specs=in_specs, out_specs=out_specs, check_vma=False)
```

```python
import functools
import math

import jax
import jax.numpy as jnp
from jax import lax
from jax.experimental import pallas as pl
from jax.experimental.pallas import tpu as pltpu
from jax.sharding import PartitionSpec as P

HEAD_DIM = 64
WINDOW = 512
REACH = 128
LANES = 128
COLS = 512

smooth = 0.1
f32 = jnp.float32
bf16 = jnp.bfloat16


def normalize(rows):
    values = rows.astype(f32)
    centre = jnp.mean(values, axis=-1, keepdims=True)
    values = values - centre
    spread = jnp.mean(values * values, axis=-1, keepdims=True)
    return (values * lax.rsqrt(spread + 1e-05)).astype(bf16)


def place_columns(mixed, scale):
    side = 256
    down = lax.broadcasted_iota(jnp.int32, (side, side), 0) >> 6
    across = lax.broadcasted_iota(jnp.int32, (side, side), 1) >> 6
    same = jnp.where(down == across, 1.0 / HEAD_DIM, 0.0).astype(bf16)
    pieces = []
    for at in range(0, mixed.shape[1], side):
        piece = mixed[:, at : at + side]
        mean = jnp.dot((piece * piece).astype(bf16), same, preferred_element_type=f32)
        pieces.append((piece * (lax.rsqrt(mean + 1e-06) * scale)).astype(bf16))
    return jnp.concatenate(pieces, axis=1)


def project(normed, weight, out, first, waits):
    width = weight.shape[0]
    for at in range(first, weight.shape[1], COLS):
        if waits:
            waits[at // COLS].wait()
        mixed = jnp.dot(normed[...], weight[:, at : at + COLS], preferred_element_type=f32)
        if at < 2 * width:
            mixed = place_columns(mixed, HEAD_DIM**-0.5 if at < width else 1.0)
        out[:, at - first : at - first + COLS] = mixed.astype(bf16)


def attend(index, own, side, joint, attended, mapped, keys, values, there):
    half = WINDOW // 2
    rows, width = attended.shape
    first = lax.broadcasted_iota(jnp.int32, (1, LANES), 1) < HEAD_DIM
    block = half
    part_rows = block // 2
    part_span = part_rows + WINDOW
    down = lax.broadcasted_iota(jnp.int32, (part_rows, part_rows), 0)
    across = lax.broadcasted_iota(jnp.int32, (part_rows, part_rows), 1)
    late = across >= down
    start = index * block
    outside = pl.ds(index * half, half)
    shift = (half, 0)[index]
    apart = (0, rows)[index]
    there = jnp.where(there, 1.0, 0.0).astype(f32)

    @pl.loop(0, width // LANES)
    def _(j):
        def at(offset):
            return pl.ds(pl.multiple_of(j * LANES + offset, LANES), LANES)

        keys[shift : shift + rows, :] = own[:, at(width)]
        keys[apart : apart + half, :] = side[outside, at(0)]
        chunks = (
            (shift, own[:, at(2 * width)], 1.0),
            (apart, side[outside, at(width)], there),
        )
        for begin, part, real in chunks:
            ones = jnp.full(part.shape, real, f32).astype(bf16)
            values[0, begin : begin + part.shape[0], :] = jnp.where(first, part, ones)
            values[1, begin : begin + part.shape[0], :] = jnp.where(first, ones, part)
        query = own[start : start + block, at(0)]
        here = keys[...]
        sums = []
        for head in range(2):
            part = jnp.where(first == (head == 0), query, jnp.zeros_like(query))
            scores = lax.dot_general(
                part, here, (((1,), (1,)), ((), ())), preferred_element_type=f32
            )
            lines = []
            for line in range(2):
                begin = line * part_rows
                weights = jnp.exp(
                    scores[begin : begin + part_rows, begin : begin + part_span]
                )
                blank = jnp.zeros((part_rows, part_rows), bf16)
                pieces = [
                    jnp.where(late, weights[:, :part_rows], 0.0).astype(bf16),
                    weights[:, part_rows : part_span - part_rows].astype(bf16),
                    jnp.where(late, 0.0, weights[:, part_span - part_rows :]).astype(bf16),
                ]
                pieces = pieces + [blank] if line == 0 else [blank] + pieces
                lines.append(jnp.concatenate(pieces, axis=1))
            total = jnp.dot(
                jnp.concatenate(lines, axis=0),
                values[head],
                preferred_element_type=f32,
            )
            sums.append(total)
        shared = pltpu.roll(jnp.where(first, sums[1], sums[0]), HEAD_DIM, 1)
        result = (jnp.where(first, sums[0], sums[1]) / shared).astype(bf16)
        attended[start : start + block, at(0)] = result
        mapped[start : start + block, :] += jnp.dot(
            result, joint[at(0), :], preferred_element_type=f32
        )


def slope(diff):
    return diff * lax.rsqrt(diff * diff + smooth * smooth)


def copy_to(source, target, send, arrive, seq, member):
    return pltpu.make_async_remote_copy(
        src_ref=source,
        dst_ref=target,
        send_sem=send,
        recv_sem=arrive,
        device_id={"seq": seq, "member": member},
        device_id_type=pl.DeviceIdType.MESH,
    )


def layer_kernel(
    seqs, members, decoder, neighbours, area, tokens_far, weight_far, observed_far, output_far,
    cotangent_out, rows_out, decoder_out,
    every, counts, turned, middle, edges, edges_in, terms, terms_in, sums, sums_in, mine,
    gathered_rows, gathered, tokens, attended, observed, output_weight,
    weight, normed, beside, own_parts, side_parts, mapped, keys, values, seen, joint,
    halo_send, halo_in,
    local_sem, field_send, field_in, side_send, side_in, edge_send, edge_in, term_send, term_in,
    sum_send, sum_in, row_send, row_in, all_send, all_in,
):
    s, m = lax.axis_index("seq"), lax.axis_index("member")
    peers = seqs * members
    me = s * members + m
    tok_rows, fields = mapped.shape
    fan, grid_rows = neighbours.shape
    wide = tok_rows + 2 * REACH
    width = tokens.shape[1]
    chunk = width // peers

    def peer(step):
        flat = lax.rem(me + step, peers)
        return flat // members, lax.rem(flat, members)

    barrier = pltpu.get_barrier_semaphore()

    @pl.loop(1, peers)
    def _(step):
        seq, member = peer(step)
        pl.semaphore_signal(
            barrier, inc=1, device_id={"seq": seq, "member": member},
            device_id_type=pl.DeviceIdType.MESH,
        )

    columns = weight.shape[1] // COLS
    loads = [
        pltpu.make_async_copy(far, near, local_sem.at[i])
        for i, (far, near) in enumerate(
            [(tokens_far, tokens)]
            + [
                (weight_far.at[:, pl.ds(i * COLS, COLS)], weight.at[:, pl.ds(i * COLS, COLS)])
                for i in range(columns)
            ]
            + [(output_far, output_weight), (observed_far, observed)]
        )
    ]
    for load in loads:
        load.start()
    has_left, has_right = s > 0, s < seqs - 1
    half = WINDOW // 2

    def halo_copy(to_right):
        start, land, seq = (tok_rows - half, 0, s + 1) if to_right else (0, half, s - 1)
        return copy_to(
            tokens_far.at[pl.ds(start, half), :], beside.at[pl.ds(land, half), :],
            halo_send.at[to_right], halo_in.at[to_right], seq, m,
        )

    @pl.when(jnp.logical_not(has_left))
    def _():
        beside[:half, :] = jnp.zeros((half, width), bf16)

    @pl.when(jnp.logical_not(has_right))
    def _():
        beside[half:, :] = jnp.zeros((half, width), bf16)

    pl.semaphore_wait(barrier, peers - 1)

    @pl.when(has_right)
    def _():
        halo_copy(1).start()

    @pl.when(has_left)
    def _():
        halo_copy(0).start()

    loads[0].wait()
    normed[...] = normalize(tokens[...])
    project(normed, weight, own_parts, 0, loads[1 : 1 + columns])
    loads[1 + columns].wait()
    joint[...] = jnp.dot(
        output_weight[...], decoder[...], preferred_element_type=f32
    ).astype(bf16)
    mapped[...] = jnp.dot(tokens[...], decoder[...], preferred_element_type=f32)
    base = s * tok_rows - REACH
    block = 128
    loads[2 + columns].wait()

    @pl.loop(0, grid_rows // block)
    def _(i):
        cells = pl.ds(pl.multiple_of(i * block, block), block)
        local = neighbours[:, cells] - base
        place = lax.broadcasted_iota(jnp.int32, (wide, block), 0)
        total = jnp.zeros((wide, block), f32)
        for k in range(fan):
            total += jnp.where(local[k : k + 1, :] == place, 1.0 / fan, 0.0)
        counts[:, cells] = total.astype(bf16)
        seen[:, cells] = observed[cells, :].T

    @pl.when(has_left)
    def _():
        halo_copy(0).wait_send()
        halo_copy(1).wait_recv()

    @pl.when(has_right)
    def _():
        halo_copy(1).wait_send()
        halo_copy(0).wait_recv()

    normed[...] = normalize(beside[...])
    project(normed, weight, side_parts, width, None)
    def field_copy(index, step):
        cells = pl.ds(REACH + index * half, half)
        return copy_to(
            every.at[pl.ds(0, fields), cells], every.at[pl.ds(step * fields, fields), cells],
            field_send.at[index, step], field_in.at[index, step], s, lax.rem(m + step, members),
        )

    def side_copy(side, step):
        start, land, seq = ((tok_rows, 0, s + 1), (REACH, REACH + tok_rows, s - 1))[side]
        return copy_to(
            every.at[pl.ds(0, fields), pl.ds(start, REACH)],
            every.at[pl.ds(step * fields, fields), pl.ds(land, REACH)],
            side_send.at[side, step], side_in.at[side, step], seq, lax.rem(m + step, members),
        )

    for index in range(2):
        attend(
            index, own_parts, side_parts, joint, attended, mapped, keys, values,
            (has_left, has_right)[index],
        )
        at = index * half
        every[:fields, REACH + at : REACH + at + half] = (
            mapped[at : at + half, :].T.astype(bf16)
        )
        for step in range(1, members):
            field_copy(index, step).start()

        @pl.when((has_left, has_right)[index])
        def _():
            for step in range(members):
                side_copy(1 - index, step).start()

    @pl.when(jnp.logical_not(has_left))
    def _():
        every[:, :REACH] = jnp.zeros((members * fields, REACH), bf16)
        edges_in[0] = jnp.zeros((fields, REACH), bf16)

    @pl.when(jnp.logical_not(has_right))
    def _():
        every[:, wide - REACH :] = jnp.zeros((members * fields, REACH), bf16)
        edges_in[1] = jnp.zeros((fields, REACH), bf16)

    for index in range(2):
        for step in range(1, members):
            field_copy(index, step).wait()

    @pl.when(has_left)
    def _():
        for step in range(members):
            side_copy(1, step).wait_send()
            side_copy(0, step).wait_recv()

    @pl.when(has_right)
    def _():
        for step in range(members):
            side_copy(0, step).wait_send()
            side_copy(1, step).wait_recv()

    block = 256

    @pl.loop(0, grid_rows // block)
    def _(i):
        cells = pl.ds(pl.multiple_of(i * block, block), block)
        found = jnp.dot(every[...], counts[:, cells], preferred_element_type=f32)
        mean = found[:fields, :]
        pairs = jnp.zeros((fields, block), f32)
        for step in range(members):
            pairs += slope(mean - found[step * fields : (step + 1) * fields, :])
        single = slope(mean - seen[:, cells])
        turned[:, cells] = (
            area[:, cells]
            * (single * (1.0 / members) - pairs * (1.0 / (members * (members - 1))))
        ).astype(bf16)

    def spread(start, size):
        return lax.dot_general(
            turned[...], counts[start : start + size, :], (((1,), (1,)), ((), ())),
            preferred_element_type=f32,
        )

    edges[0] = spread(0, REACH).astype(bf16)
    edges[1] = spread(REACH + tok_rows, REACH).astype(bf16)

    def edge_copy(side):
        return copy_to(
            edges.at[side], edges_in.at[1 - side], edge_send.at[side], edge_in.at[side],
            s - 1 if side == 0 else s + 1, m,
        )

    @pl.when(has_left)
    def _():
        edge_copy(0).start()

    @pl.when(has_right)
    def _():
        edge_copy(1).start()

    middle[...] = spread(REACH, tok_rows)
    inner = middle[:, REACH : tok_rows - REACH].astype(bf16)
    output_term = jnp.dot(
        inner, attended[REACH : tok_rows - REACH, :], preferred_element_type=f32
    )

    @pl.when(has_left)
    def _():
        edge_copy(0).wait_send()
        edge_copy(1).wait_recv()

    @pl.when(has_right)
    def _():
        edge_copy(1).wait_send()
        edge_copy(0).wait_recv()

    middle[:, :REACH] += edges_in[0].astype(f32)
    middle[:, tok_rows - REACH :] += edges_in[1].astype(f32)
    whole = middle[...].astype(bf16)
    output_term += jnp.dot(whole[:, :REACH], attended[:REACH, :], preferred_element_type=f32)
    output_term += jnp.dot(
        whole[:, tok_rows - REACH :], attended[tok_rows - REACH :, :],
        preferred_element_type=f32,
    )

    def put(part, value):
        rows = value.T.astype(bf16)
        for member in range(members):
            for seq in range(seqs):
                at = (seq * members + member) * chunk
                terms[part, member, seq] = rows[at : at + chunk, :]

    def term_copy(part, step):
        member = lax.rem(m + step, members)
        return copy_to(
            terms.at[part, member], terms_in.at[part, step],
            term_send.at[part, step], term_in.at[part, step], s, member,
        )

    def sum_copy(part, step):
        seq = lax.rem(s + step, seqs)
        return copy_to(
            sums.at[part, seq], sums_in.at[part, step],
            sum_send.at[part, step], sum_in.at[part, step], seq, m,
        )

    put(0, output_term)
    for step in range(1, members):
        term_copy(0, step).start()
    decoder_term = jnp.dot(whole, tokens[...], preferred_element_type=f32)
    decoder_term += jnp.dot(
        output_term.astype(bf16), output_weight[...], preferred_element_type=f32
    )
    put(1, decoder_term)
    for step in range(1, members):
        term_copy(1, step).start()
    cotangent_out[...] = lax.dot_general(
        middle[...].T.astype(bf16), joint[...], (((1,), (1,)), ((), ())),
        preferred_element_type=f32,
    ).astype(bf16)
    for part in range(2):
        for step in range(1, members):
            term_copy(part, step).wait()
        total = terms[part, m].astype(f32)
        for step in range(1, members):
            total += terms_in[part, step].astype(f32)
        sums[part] = total.astype(bf16)

        @pl.loop(1, seqs)
        def _(step):
            sum_copy(part, step).start()

    def row_copy(step):
        return copy_to(
            mine.at[0], gathered_rows.at[m], row_send.at[step], row_in.at[step],
            s, lax.rem(m + step, members),
        )

    def all_copy(step):
        seq, member = peer(step)
        return copy_to(
            mine.at[1], gathered.at[me], all_send.at[step], all_in.at[step], seq, member
        )

    for part in range(2):

        @pl.loop(1, seqs)
        def _(step):
            sum_copy(part, step).wait()

        total = sums[part, s].astype(f32)
        for step in range(1, seqs):
            total += sums_in[part, step].astype(f32)
        mine[part] = total.astype(bf16)
        if part == 0:
            for step in range(1, members):
                row_copy(step).start()
        else:

            @pl.loop(1, peers)
            def _(step):
                all_copy(step).start()

    gathered_rows[m] = mine[0]
    gathered[me] = mine[1]
    for step in range(1, members):
        row_copy(step).wait()
    rows_out[...] = gathered_rows[...]

    @pl.loop(1, peers)
    def _(step):
        all_copy(step).wait()

    decoder_out[...] = gathered[...]


def layer(decoder, neighbours, area, tokens, weight, observed, output_weight, seqs, members):
    tok_rows, width = tokens.shape
    fields = decoder.shape[1]
    grid_rows = neighbours.shape[1]
    wide = tok_rows + 2 * REACH
    peers = seqs * members
    chunk = width // peers
    near = pl.BlockSpec(memory_space=pltpu.VMEM)
    far = pl.BlockSpec(memory_space=pl.ANY)
    dma = pltpu.SemaphoreType.DMA
    return pl.pallas_call(
        functools.partial(layer_kernel, seqs, members),
        in_specs=[near] * 3 + [far] * 4,
        out_specs=[near] * 3,
        out_shape=[
            jax.ShapeDtypeStruct((tok_rows, width), bf16),
            jax.ShapeDtypeStruct((members, chunk, fields), bf16),
            jax.ShapeDtypeStruct((peers, chunk, fields), bf16),
        ],
        scratch_shapes=[
            pltpu.VMEM((members * fields, wide), bf16),
            pltpu.VMEM((wide, grid_rows), bf16),
            pltpu.VMEM((fields, grid_rows), bf16),
            pltpu.VMEM((fields, tok_rows), f32),
            pltpu.VMEM((2, fields, REACH), bf16),
            pltpu.VMEM((2, fields, REACH), bf16),
            pltpu.VMEM((2, members, seqs, chunk, fields), bf16),
            pltpu.VMEM((2, members, seqs, chunk, fields), bf16),
            pltpu.VMEM((2, seqs, chunk, fields), bf16),
            pltpu.VMEM((2, seqs, chunk, fields), bf16),
            pltpu.VMEM((2, chunk, fields), bf16),
            pltpu.VMEM((members, chunk, fields), bf16),
            pltpu.VMEM((peers, chunk, fields), bf16),
            pltpu.VMEM(tokens.shape, bf16),
            pltpu.VMEM(tokens.shape, bf16),
            pltpu.VMEM(observed.shape, f32),
            pltpu.VMEM(output_weight.shape, bf16),
            pltpu.VMEM(weight.shape, bf16),
            pltpu.VMEM(tokens.shape, bf16),
            pltpu.VMEM((WINDOW, width), bf16),
            pltpu.VMEM((tok_rows, 3 * width), bf16),
            pltpu.VMEM((WINDOW, 2 * width), bf16),
            pltpu.VMEM((tok_rows, fields), f32),
            pltpu.VMEM((WINDOW // 2 + WINDOW, LANES), bf16),
            pltpu.VMEM((2, WINDOW // 2 + WINDOW, LANES), bf16),
            pltpu.VMEM((fields, grid_rows), f32),
            pltpu.VMEM((width, fields), bf16),
            dma((2,)),
            dma((2,)),
            dma((3 + weight.shape[1] // COLS,)),
            dma((2, members)),
            dma((2, members)),
            dma((2, members)),
            dma((2, members)),
            dma((2,)),
            dma((2,)),
            dma((2, members)),
            dma((2, members)),
            dma((2, seqs)),
            dma((2, seqs)),
            dma((members,)),
            dma((members,)),
            dma((peers,)),
            dma((peers,)),
        ],
        compiler_params=pltpu.CompilerParams(
            vmem_limit_bytes=56 << 20, collective_id=0, has_side_effects=True
        ),
    )(decoder, neighbours, area, tokens, weight, observed, output_weight)


def body(tokens, input_weight, output_weight, decoder_weight, neighbours, observed, cell_area):
    own_tokens = tokens[0]
    tok_rows, width = own_tokens.shape
    fields = decoder_weight.shape[1]
    seqs = lax.axis_size("seq")
    members = lax.axis_size("member")
    grid_rows = neighbours.shape[0]
    attention_cotangent, rows, decoder_sum = layer(
        decoder_weight, neighbours.T, cell_area[None, :], own_tokens, input_weight, observed,
        output_weight, seqs, members,
    )
    output_gradient = lax.dot_general(
        rows.reshape(width // seqs, fields), decoder_weight, (((1,), (1,)), ((), ())),
        preferred_element_type=f32,
    ) * (1.0 / math.sqrt(members * tok_rows * seqs))
    decoder_gradient = decoder_sum.reshape(width, fields).astype(f32) * (
        1.0 / math.sqrt(members * grid_rows * seqs)
    )
    return (attention_cotangent[None], output_gradient, decoder_gradient)


def solution(mesh):
    in_specs = (
        P(("group", "member"), "seq", None),
        P(),
        P(),
        P(),
        P("seq", None),
        P(("group", "seq"), None),
        P("seq"),
    )
    out_specs = (P(("group", "member"), "seq", None), P(("group", "seq"), None), P("group", None))
    return jax.shard_map(body, mesh=mesh, in_specs=in_specs, out_specs=out_specs, check_vma=False)
```
